128 devices in a mesh: obs: 8 (over x, core), flux: 16 (over z, y).
Axes of the slice: x: 4, y: 4, z: 4, core: 2. Of those that a mesh axis runs over, the one named last changes fastest.
Arguments:
- probes: bfloat16 [768, 32, 128], P('flux'), may hold values from -6 to 6
- prior_tiles: bfloat16 [768, 8, 128, 128], P('flux'), may hold values from -0.1875 to 0.1875
- neighbours: int32 [768, 8], P('flux'), may hold values from 0 to 767, as said below
- jac: bfloat16 [8, 16, 384, 128, 128], P('obs', 'flux'), may hold values from -0.0390625 to 0.0390625
- jac_obs: int32 [8, 16, 384], P('obs', 'flux'), may hold values from 0 to 31
- jac_flux: int32 [8, 16, 384], P('obs', 'flux'), may hold values from 0 to 47
- counts: int32 [8, 16], P('obs', 'flux'), may hold values from 96 to 384
- rinv: float32 [256, 128], P('obs'), may hold values from 0.25 to 2.5
Outputs:
- power: bfloat16 [768, 32, 128], P('flux')
The draws below stay inside these ranges and needn't reach their ends.
Inputs may be any that keep to these rules, and one draw needn't show every extreme that they name: `neighbours`: every entry lies within 12 tiles of its own tile t, and entry 0 is t itself.
All inputs are finite; a program needn't handle non-finite values.
Results may differ from the reference program's by a relative error of at most 0.024.
Values may be sent and summed in bfloat16 or wider, within the bound.
A program may use at most 128 MiB of HBM per device.

```python
import math
import jax
import jax.numpy as jnp
from jax import lax

BLK = 128
PROBES = 32
NBRS = 8
STEPS = 4
FB_DEV = 48
OB_DEV = 32
NB_DEV = 384
REACH = 12
FB = 768
OBLK = 256
N_OBS = 8
N_FLUX = 16


def draw_neighbours(key, part):
    key_sign = jax.random.fold_in(key, 11)
    key_offset = jax.random.fold_in(key, 12)
    tiles = jnp.arange(FB, dtype=jnp.int32)[:, None]
    signs = jax.random.randint(key_sign, (FB, 1), 0, 2).astype(jnp.int32) * 2 - 1
    offsets = jax.random.randint(key_offset, (FB, NBRS - 2), -REACH, REACH + 1).astype(jnp.int32)
    columns = jnp.concatenate([jnp.zeros((FB, 1), jnp.int32), signs * REACH, offsets], axis=1)
    return jnp.clip(tiles + columns, 0, FB - 1).astype(jnp.int32)


def draw_counts(key, part):
    key_count = jax.random.fold_in(key, 21)
    key_place = jax.random.fold_in(key, 22)
    values = jax.random.randint(key_count, (N_OBS * N_FLUX,), NB_DEV // 4, NB_DEV + 1).astype(jnp.int32)
    place = jax.random.randint(key_place, (), 0, N_OBS * N_FLUX).astype(jnp.int32)
    values = jnp.where(jnp.arange(N_OBS * N_FLUX, dtype=jnp.int32) == place, NB_DEV, values)
    return values.reshape(N_OBS, N_FLUX).astype(jnp.int32)


def set_ends(result, stream_key, least, high):
    extent = result.shape
    spot = [jax.random.randint(jax.random.fold_in(stream_key, axis), (), 0, extent[axis]) for axis in range(len(extent))]
    result = result.at[tuple(spot)].set(least)
    longest = extent.index(max(extent))
    spot[longest] = (spot[longest] + 1) % extent[longest]
    return result.at[tuple(spot)].set(high)


def block_scale(key, extent, shards, smallest, largest):
    factor_of = 1.0
    for axis_at, blocks in shards:
        heights = jax.random.uniform(jax.random.fold_in(jax.random.fold_in(key, 6), axis_at), (blocks,), jnp.float32, smallest / len(shards), largest / len(shards))
        factor_of = factor_of * jnp.repeat(jnp.exp(heights), extent[axis_at] // blocks).reshape((-1,) + (1,) * (len(extent) - 1 - axis_at))
    return factor_of


def gaussian(rng, extent, scale, most, cuts=(), held_as=jnp.bfloat16):
    values = jax.random.normal(rng, extent, jnp.float32) * scale
    if len(cuts) > 0:
        values = block_scale(rng, extent, cuts, -0.22, 0.18) * values
    return jnp.clip(values, min=-most, max=most).astype(held_as)


def setup_inputs(seed: int = 0) -> dict:
    key_of = jax.random.split(jax.random.key(seed), 9)
    return {
        "probes": gaussian(key_of[0], (FB, PROBES, BLK), 1.0, 6.0, ((0, 16),)),
        "prior_tiles": gaussian(key_of[1], (FB, NBRS, BLK, BLK), (BLK * NBRS) ** -0.5, 0.1875, ((0, 16),)),
        "neighbours": draw_neighbours(jax.random.fold_in(key_of[8], 71), 0),
        "jac": gaussian(key_of[3], (N_OBS, N_FLUX, NB_DEV, BLK, BLK), (BLK * NB_DEV * N_FLUX // OB_DEV) ** -0.5, 0.0390625, ((0, 8), (1, 16))),
        "jac_obs": set_ends(jax.random.randint(key_of[4], (N_OBS, N_FLUX, NB_DEV), 0, OB_DEV), jax.random.fold_in(key_of[4], 1), 0, OB_DEV - 1).astype(jnp.int32),
        "jac_flux": set_ends(jax.random.randint(key_of[5], (N_OBS, N_FLUX, NB_DEV), 0, FB_DEV), jax.random.fold_in(key_of[5], 1), 0, FB_DEV - 1).astype(jnp.int32),
        "counts": draw_counts(jax.random.fold_in(key_of[8], 71), 0),
        "rinv": jnp.clip(jnp.exp(math.log(2.5) - 2.3025851 * jax.random.uniform(key_of[7], (OBLK, BLK), jnp.float32) ** block_scale(key_of[7], (OBLK, BLK), ((0, 8),), -0.2, 0.2)), 0.25, 2.5),
    }


def reference(probes, prior_tiles, neighbours, jac, jac_obs, jac_flux, counts, rinv):
    f32 = jnp.float32
    half = jnp.bfloat16
    prior_grouped = prior_tiles.reshape(N_FLUX, FB_DEV, NBRS, BLK, BLK)
    nbr_grouped = neighbours.reshape(N_FLUX, FB_DEV, NBRS)
    flux_groups = jnp.arange(N_FLUX, dtype=jnp.int32)
    all_groups = jnp.arange(N_OBS * N_FLUX, dtype=jnp.int32)
    slots = jnp.arange(NB_DEV, dtype=jnp.int32)
    obs_range = jnp.arange(OB_DEV, dtype=jnp.int32)
    tile_range = jnp.arange(FB_DEV, dtype=jnp.int32)

    def prior_forward(field):
        def one(group):
            picked = field[nbr_grouped[group]]
            return jnp.einsum("tkpc,tkcd->tpd", picked.astype(f32), prior_grouped[group].astype(f32))
        return lax.map(one, flux_groups).reshape(FB, PROBES, BLK).astype(half)

    def prior_adjoint(field):
        grouped = field.reshape(N_FLUX, FB_DEV, PROBES, BLK)

        def one(carry, group):
            contrib = jnp.einsum("tpd,tkcd->tkpc", grouped[group].astype(f32), prior_grouped[group].astype(f32))
            carry = carry.at[nbr_grouped[group].reshape(-1)].add(contrib.reshape(-1, PROBES, BLK))
            return carry, None
        total, unused = lax.scan(one, jnp.zeros((FB, PROBES, BLK), f32), flux_groups)
        return total.astype(half)

    def forward(spread):
        def one(group):
            row = group // N_FLUX
            col = group % N_FLUX
            live = (slots < counts[row, col]).astype(f32)
            shard = lax.dynamic_slice_in_dim(spread, (col * FB_DEV).astype(jnp.int32), FB_DEV, 0)
            picked = shard[jac_flux[row, col]]
            prod = jnp.einsum("npc,nco->npo", picked.astype(f32), jac[row, col].astype(f32))
            hot = (jac_obs[row, col][None, :] == obs_range[:, None]).astype(f32) * live[None, :]
            return jnp.einsum("bn,npo->bpo", hot, prod)
        parts = lax.map(one, all_groups).reshape(N_OBS, N_FLUX, OB_DEV, PROBES, BLK)
        return jnp.sum(parts, axis=1).reshape(OBLK, PROBES, BLK)

    def adjoint(weighted):
        def one(group):
            row = group // N_FLUX
            col = group % N_FLUX
            live = (slots < counts[row, col]).astype(f32)
            shard = lax.dynamic_slice_in_dim(weighted, (row * OB_DEV).astype(jnp.int32), OB_DEV, 0)
            picked = shard[jac_obs[row, col]]
            prod = jnp.einsum("npo,nco->npc", picked.astype(f32), jac[row, col].astype(f32))
            hot = (jac_flux[row, col][None, :] == tile_range[:, None]).astype(f32) * live[None, :]
            return jnp.einsum("tn,npc->tpc", hot, prod)
        parts = lax.map(one, all_groups).reshape(N_OBS, N_FLUX, FB_DEV, PROBES, BLK)
        return jnp.sum(parts, axis=0).reshape(FB, PROBES, BLK).astype(half)

    field = probes
    for step in range(STEPS):
        spread = prior_forward(field)
        predicted = forward(spread)
        weighted = (predicted * rinv[:, None, :]).astype(half)
        back = adjoint(weighted)
        field = prior_adjoint(back)
    return field
```

```python
import functools

import jax
import jax.numpy as jnp
from jax import lax
from jax.experimental import pallas as pl
from jax.experimental.pallas import tpu as pltpu
from jax.sharding import PartitionSpec as P

STEPS = 4
REACH = 12
SIDE = 2
MESH = pl.DeviceIdType.MESH
F32 = jnp.float32
BF16 = jnp.bfloat16


def segment_pairs(key, lhs, segments, zero_lhs, pairs):
    count = key.shape[0]
    order = jnp.arange(count, dtype=jnp.int32)
    names = jnp.arange(segments, dtype=jnp.int32)
    hot = (key[:, None] == names[None, :]).astype(jnp.int32)
    size = jnp.sum(hot, axis=0)
    even = (size + 1) // 2 * 2
    begin = jnp.sum(jnp.where(names[None, :] < names[:, None], even[None, :], 0), axis=1)
    same = (key[None, :] == key[:, None]) & (order[None, :] < order[:, None])
    rank = jnp.sum(same.astype(jnp.int32), axis=1)
    place = jnp.where(key < segments, jnp.sum(hot * begin[None, :], axis=1) + rank, -1)
    slots = jnp.arange(2 * pairs, dtype=jnp.int32)
    match = slots[:, None] == place[None, :]
    block = jnp.sum(jnp.where(match, order[None, :], 0), axis=1)
    left = zero_lhs + jnp.sum(jnp.where(match, lhs[None, :] - zero_lhs, 0), axis=1)
    opens = (slots[::2][:, None] == begin[None, :]) & (size > 0)[None, :]
    flag = 1 - jnp.sum(opens.astype(jnp.int32), axis=1)
    last = jnp.where(size > 0, (begin + even) // 2 - 1, pairs)
    return jnp.concatenate([block, left, flag, last]).astype(jnp.int32)


def unroll_of(total, most):
    return max(u for u in range(1, most + 1) if total % u == 0)


def kernel(
    g, idx, probes, prior, jac, rinv, out,
    blocks, flipped, prior_own, prior_flip, ext, spread, weighted, adjoint, scan,
    part_obs, got_obs, part_cell, got_cell, part_field, got_field,
    load_sem, fs, fr, ws, wr, os_, or_, gs, gr, cs, cr, es, er,
):
    no, nf, chunk = g["no"], g["nf"], g["chunk"]
    tiles, obs_blocks, nbrs, slots = g["tiles"], g["obs_blocks"], g["nbrs"], g["slots"]
    mine = obs_blocks // nf
    reach = (2 * SIDE + 1) * chunk
    o = lax.axis_index("obs")
    f = lax.axis_index("flux")
    chunks = no * nf

    def chunk_of(o_, f_):
        odd = lax.rem(f_, 2)
        return odd * (no - 1 - o_) + (1 - odd) * o_

    c = chunk_of(o, f)
    q = f * no + c

    def holder(distance):
        at = lax.rem(q + distance + chunks, chunks)
        f_ = lax.div(at, no)
        return (chunk_of(lax.rem(at, no), f_), f_)

    def flux_peer(r):
        return (o, lax.rem(f + r, nf))

    def obs_peer(r):
        return (lax.rem(o + r, no), f)

    sides = [d for d in range(-SIDE, SIDE + 1) if d != 0]

    load_jac = pltpu.make_async_copy(jac, blocks, load_sem.at[0])
    load_prior = pltpu.make_async_copy(prior.at[pl.ds(c * chunk, chunk)], prior_own, load_sem.at[1])
    load_field = pltpu.make_async_copy(
        probes.at[pl.ds(c * chunk, chunk)], ext.at[pl.ds(SIDE * chunk, chunk)], load_sem.at[2]
    )
    load_field.start()
    load_prior.start()
    load_jac.start()

    barrier = pltpu.get_barrier_semaphore()
    partners = [flux_peer(r) for r in range(1, nf)] + [obs_peer(r) for r in range(1, no)]
    partners += [holder(d) for d in sides]
    for partner in partners:
        pl.semaphore_signal(barrier, inc=1, device_id=partner, device_id_type=MESH)
    pl.semaphore_wait(barrier, len(partners))

    zero = jnp.zeros(spread.shape[1:], BF16)
    spread[tiles] = zero
    weighted[obs_blocks] = zero
    adjoint[chunk] = zero

    def remote(src, dst, send, recv, device):
        return pltpu.make_async_remote_copy(
            src_ref=src, dst_ref=dst, send_sem=send, recv_sem=recv, device_id=device, device_id_type=MESH
        )

    def start_all(copies):
        for copy in copies:
            copy.start()

    def wait_all(copies):
        for copy in copies:
            copy.wait_recv()
        for copy in copies:
            copy.wait_send()

    def products(base, pairs, lhs_ref, rhs_ref, unroll):
        def one(m, acc):
            a, b = base + 2 * m, base + 2 * m + 1
            left = jnp.concatenate([lhs_ref[idx[2 * pairs + a]], lhs_ref[idx[2 * pairs + b]]], axis=1)
            right = jnp.concatenate([rhs_ref[idx[a]], rhs_ref[idx[b]]], axis=0)
            acc = acc * idx[base + 4 * pairs + m].astype(F32)
            acc = acc + jnp.dot(left, right, preferred_element_type=F32)
            scan[m] = acc
            return acc

        def some(i, acc):
            for u in range(unroll):
                acc = one(i * unroll + u, acc)
            return acc

        lax.fori_loop(0, pairs // unroll, some, jnp.zeros(scan.shape[1:], F32))
        scan[pairs] = jnp.zeros(scan.shape[1:], F32)
        return base + 5 * pairs

    def field_copies():
        own = ext.at[pl.ds(SIDE * chunk, chunk)]
        return [
            remote(own, ext.at[pl.ds((SIDE - d) * chunk, chunk)], es.at[i], er.at[i], holder(d))
            for i, d in enumerate(sides)
        ]

    def gather_copies():
        own = spread.at[pl.ds(c * chunk, chunk)]
        return [remote(own, own, gs.at[r - 1], gr.at[r - 1], obs_peer(r)) for r in range(1, no)]

    load_field.wait()

    def step(s, carry):
        copies = field_copies()
        start_all(copies)

        @pl.when(s == 0)
        def _():
            load_prior.wait()

        wait_all(copies)

        def spread_one(t, carry):
            left = jnp.concatenate([ext[idx[g["nbr_at"] + t * nbrs + k]] for k in range(nbrs)], axis=1)
            right = prior_own[t].reshape(nbrs * prior_own.shape[2], prior_own.shape[3])
            spread[c * chunk + t] = jnp.dot(left, right, preferred_element_type=F32).astype(BF16)
            return carry

        for t in range(chunk):
            spread_one(t, 0)
        copies = gather_copies()
        start_all(copies)

        @pl.when(s == 0)
        def _():
            load_jac.wait()

            def flip(e, carry):
                t, k = e // nbrs, e % nbrs
                prior_flip[e] = prior_own[t, k].T
                return carry

            for e in range(chunk * nbrs):
                flip(e, 0)

        wait_all(copies)

        last = products(g["fwd_at"], g["fwd_pairs"], spread, blocks, g["fwd_unroll"])
        for b in range(obs_blocks):
            part_obs[b] = scan[idx[last + b]].astype(BF16)
        copies = []
        for r in range(1, nf):
            peer = flux_peer(r)
            copies.append(
                remote(part_obs.at[pl.ds(peer[1] * mine, mine)], got_obs.at[r - 1], fs.at[r - 1], fr.at[r - 1], peer)
            )
        start_all(copies)

        @pl.when(s == 0)
        def _():
            many = unroll_of(slots, 8)

            def flip(i, carry):
                for u in range(many):
                    flipped[i * many + u] = blocks[i * many + u].T
                return carry

            lax.fori_loop(0, slots // many, flip, 0)

        wait_all(copies)
        for b in range(mine):
            total = scan[idx[last + f * mine + b]]
            for r in range(1, nf):
                total = total + got_obs[r - 1, b].astype(F32)
            weighted[f * mine + b] = (total * rinv[pl.ds(f * mine + b, 1), :]).astype(BF16)
        own = weighted.at[pl.ds(f * mine, mine)]
        copies = [remote(own, own, ws.at[r - 1], wr.at[r - 1], flux_peer(r)) for r in range(1, nf)]
        start_all(copies)
        wait_all(copies)

        last = products(g["adj_at"], g["adj_pairs"], weighted, flipped, g["adj_unroll"])
        for t in range(tiles):
            part_cell[t] = scan[idx[last + t]].astype(BF16)
        copies = []
        for r in range(1, no):
            peer = obs_peer(r)
            at = chunk_of(peer[0], f) * chunk
            copies.append(
                remote(part_cell.at[pl.ds(at, chunk)], got_cell.at[r - 1], os_.at[r - 1], or_.at[r - 1], peer)
            )
        start_all(copies)
        wait_all(copies)
        for t in range(chunk):
            total = scan[idx[last + c * chunk + t]]
            for r in range(1, no):
                total = total + got_cell[r - 1, t].astype(F32)
            adjoint[t] = total.astype(BF16)

        last = products(g["gat_at"], g["gat_pairs"], adjoint, prior_flip, g["gat_unroll"])
        for j in range(reach):
            if j // chunk != SIDE:
                part_field[j] = scan[idx[last + j]].astype(BF16)
        copies = [
            remote(part_field.at[pl.ds((SIDE + d) * chunk, chunk)], got_field.at[i], cs.at[i], cr.at[i], holder(d))
            for i, d in enumerate(sides)
        ]
        start_all(copies)
        wait_all(copies)
        for t in range(chunk):
            total = scan[idx[last + SIDE * chunk + t]]
            for i in range(len(sides)):
                total = total + got_field[i, t].astype(F32)
            ext[SIDE * chunk + t] = total.astype(BF16)
        return carry

    lax.fori_loop(0, STEPS, step, 0)
    for t in range(chunk):
        spread[c * chunk + t] = ext[SIDE * chunk + t]
    copies = gather_copies()
    start_all(copies)
    wait_all(copies)
    out[...] = spread[pl.ds(0, tiles)]


def shards(no, nf, probes, prior_tiles, neighbours, jac, jac_obs, jac_flux, counts, rinv):
    tiles, probe_count, width = probes.shape
    nbrs = prior_tiles.shape[1]
    obs_blocks = rinv.shape[0]
    slots = jac.shape[2]
    chunk = tiles // no
    assert SIDE * chunk == REACH and obs_blocks % nf == 0
    reach = (2 * SIDE + 1) * chunk
    fwd_pairs = (slots + obs_blocks) // 2
    adj_pairs = (slots + tiles) // 2
    gat_pairs = (chunk * nbrs + reach) // 2
    o = lax.axis_index("obs")
    f = lax.axis_index("flux")
    c = jnp.where(f % 2 == 1, no - 1 - o, o)
    live = jnp.arange(slots, dtype=jnp.int32) < counts[0, 0]
    block_obs, block_flux = jac_obs[0, 0], jac_flux[0, 0]
    own = lax.dynamic_slice_in_dim(neighbours, c * chunk, chunk, 0).reshape(-1)
    own = own - (f * tiles + c * chunk - SIDE * chunk)
    entry_tile = jnp.arange(chunk * nbrs, dtype=jnp.int32) // nbrs
    fwd = segment_pairs(jnp.where(live, block_obs, obs_blocks), block_flux, obs_blocks, tiles, fwd_pairs)
    adj = segment_pairs(jnp.where(live, block_flux, tiles), block_obs, tiles, obs_blocks, adj_pairs)
    gat = segment_pairs(own, entry_tile, reach, chunk, gat_pairs)
    idx = jnp.concatenate([fwd, adj, gat, own])
    g = dict(
        no=no, nf=nf, chunk=chunk, tiles=tiles, obs_blocks=obs_blocks, nbrs=nbrs, slots=slots,
        fwd_pairs=fwd_pairs, adj_pairs=adj_pairs, gat_pairs=gat_pairs,
        fwd_at=0, adj_at=fwd.shape[0], gat_at=fwd.shape[0] + adj.shape[0],
        nbr_at=fwd.shape[0] + adj.shape[0] + gat.shape[0],
        fwd_unroll=unroll_of(fwd_pairs, 56), adj_unroll=unroll_of(adj_pairs, 56),
        gat_unroll=unroll_of(gat_pairs, 56),
    )
    mine = obs_blocks // nf
    tile = (probe_count, width)
    dma = pltpu.SemaphoreType.DMA
    most = max(fwd_pairs, adj_pairs, gat_pairs) + 1
    vmem = pl.BlockSpec(memory_space=pltpu.VMEM)
    any_space = pl.BlockSpec(memory_space=pl.ANY)
    return pl.pallas_call(
        functools.partial(kernel, g),
        out_shape=jax.ShapeDtypeStruct((tiles,) + tile, BF16),
        in_specs=[pl.BlockSpec(memory_space=pltpu.SMEM), any_space, any_space, any_space, vmem],
        out_specs=vmem,
        scratch_shapes=[
            pltpu.VMEM((slots, width, width), BF16),
            pltpu.VMEM((slots, width, width), BF16),
            pltpu.VMEM((chunk, nbrs, width, width), BF16),
            pltpu.VMEM((chunk * nbrs, width, width), BF16),
            pltpu.VMEM((reach,) + tile, BF16),
            pltpu.VMEM((tiles + 1,) + tile, BF16),
            pltpu.VMEM((obs_blocks + 1,) + tile, BF16),
            pltpu.VMEM((chunk + 1,) + tile, BF16),
            pltpu.VMEM((most,) + tile, F32),
            pltpu.VMEM((obs_blocks,) + tile, BF16),
            pltpu.VMEM((nf - 1, mine) + tile, BF16),
            pltpu.VMEM((tiles,) + tile, BF16),
            pltpu.VMEM((no - 1, chunk) + tile, BF16),
            pltpu.VMEM((reach,) + tile, BF16),
            pltpu.VMEM((2 * SIDE, chunk) + tile, BF16),
            dma((3,)),
            dma((nf - 1,)), dma((nf - 1,)), dma((nf - 1,)), dma((nf - 1,)),
            dma((no - 1,)), dma((no - 1,)), dma((no - 1,)), dma((no - 1,)),
            dma((2 * SIDE,)), dma((2 * SIDE,)), dma((2 * SIDE,)), dma((2 * SIDE,)),
        ],
        compiler_params=pltpu.CompilerParams(
            collective_id=0, has_side_effects=True, vmem_limit_bytes=48 * 1024 * 1024
        ),
    )(idx, probes, prior_tiles, jac[0, 0], rinv)


def solution(mesh):
    placed = (
        P("flux", None, None),
        P("flux", None, None, None),
        P("flux", None),
        P("obs", "flux", None, None, None),
        P("obs", "flux", None),
        P("obs", "flux", None),
        P("obs", "flux"),
        P("obs", None),
    )
    return jax.shard_map(
        functools.partial(shards, mesh.shape["obs"], mesh.shape["flux"]),
        mesh=mesh, in_specs=placed, out_specs=P("flux", None, None), check_vma=False,
    )
```

```python
import functools

import jax
import jax.numpy as jnp
from jax import lax
from jax.experimental import pallas as pl
from jax.experimental.pallas import tpu as pltpu
from jax.sharding import PartitionSpec as P

STEPS = 4
REACH = 12
FLUX_MINOR = 4
SIDE = 2
MESH = pl.DeviceIdType.MESH
F32 = jnp.float32
BF16 = jnp.bfloat16


def segment_pairs(key, lhs, segments, zero_lhs, pairs):
    count = key.shape[0]
    order = jnp.arange(count, dtype=jnp.int32)
    names = jnp.arange(segments, dtype=jnp.int32)
    hot = (key[:, None] == names[None, :]).astype(jnp.int32)
    size = jnp.sum(hot, axis=0)
    even = (size + 1) // 2 * 2
    begin = jnp.sum(jnp.where(names[None, :] < names[:, None], even[None, :], 0), axis=1)
    same = (key[None, :] == key[:, None]) & (order[None, :] < order[:, None])
    rank = jnp.sum(same.astype(jnp.int32), axis=1)
    place = jnp.where(key < segments, jnp.sum(hot * begin[None, :], axis=1) + rank, -1)
    slots = jnp.arange(2 * pairs, dtype=jnp.int32)
    match = slots[:, None] == place[None, :]
    block = jnp.sum(jnp.where(match, order[None, :], 0), axis=1)
    left = zero_lhs + jnp.sum(jnp.where(match, lhs[None, :] - zero_lhs, 0), axis=1)
    opens = (slots[::2][:, None] == begin[None, :]) & (size > 0)[None, :]
    flag = 1 - jnp.sum(opens.astype(jnp.int32), axis=1)
    last = jnp.where(size > 0, (begin + even) // 2 - 1, pairs)
    return jnp.concatenate([block, left, flag, last]).astype(jnp.int32)


def unroll_of(total, most):
    return max(u for u in range(1, most + 1) if total % u == 0)


def kernel(
    g, idx, probes, prior, jac, rinv, out,
    blocks, flipped, prior_own, prior_flip, ext_a, ext_b, spread_a, spread_b, weighted_a, weighted_b, adjoint_a, adjoint_b, scan,
    part_obs, got_obs, part_cell, got_cell, part_field, got_field,
    load_sem, fs, fr, ws, wr, os_, or_, gs, gr, cs, cr, es, er,
):
    no, nf, chunk = g["no"], g["nf"], g["chunk"]
    tiles, obs_blocks, nbrs, slots = g["tiles"], g["obs_blocks"], g["nbrs"], g["slots"]
    mine = obs_blocks // nf
    reach = (2 * SIDE + 1) * chunk
    ext, spread = (ext_a, ext_b), (spread_a, spread_b)
    weighted, adjoint = (weighted_a, weighted_b), (adjoint_a, adjoint_b)
    rows = ext_a.shape[1]
    o = lax.axis_index("obs")
    f = lax.axis_index("flux")
    chunks = no * nf

    def chunk_of(o_, f_):
        odd = lax.rem(f_, 2)
        return odd * (no - 1 - o_) + (1 - odd) * o_

    c = chunk_of(o, f)
    q = f * no + c

    def holder(distance):
        at = lax.rem(q + distance + chunks, chunks)
        f_ = lax.div(at, no)
        return (chunk_of(lax.rem(at, no), f_), f_)

    def flux_peer(r):
        y = g["flux_minor"]
        dz, dy = r
        z_ = lax.rem(lax.div(f, y) + dz, nf // y)
        y_ = lax.rem(lax.rem(f, y) + dy, y)
        return (o, z_ * y + y_)

    def obs_peer(r):
        return (lax.rem(o + r, no), f)

    def hops(d, n):
        return min(d, n - d)

    y = g["flux_minor"]
    far = [(dz, dy) for dz in range(nf // y) for dy in range(y) if dz + dy > 0]
    far.sort(key=lambda r: (-hops(r[0], nf // y) - hops(r[1], y), r))
    around = sorted(range(1, no), key=lambda r: (-hops(r, no), r))
    sides = [d for d in range(-SIDE, SIDE + 1) if d != 0]

    load_jac = pltpu.make_async_copy(jac, blocks, load_sem.at[0])
    load_prior = pltpu.make_async_copy(prior.at[pl.ds(c * chunk, chunk)], prior_own, load_sem.at[1])
    load_field = [
        pltpu.make_async_copy(
            probes.at[pl.ds(c * chunk, chunk), pl.ds(h * rows, rows)],
            ext[h].at[pl.ds(SIDE * chunk, chunk)], load_sem.at[2 + h],
        )
        for h in range(2)
    ]
    for copy in load_field:
        copy.start()
    load_prior.start()
    load_jac.start()

    barrier = pltpu.get_barrier_semaphore()
    partners = [flux_peer(r) for r in far] + [obs_peer(r) for r in around]
    partners += [holder(d) for d in sides]
    for partner in partners:
        pl.semaphore_signal(barrier, inc=1, device_id=partner, device_id_type=MESH)
    pl.semaphore_wait(barrier, len(partners))

    zero = jnp.zeros(spread_a.shape[1:], BF16)
    for h in range(2):
        spread[h][tiles] = zero
        weighted[h][obs_blocks] = zero
        adjoint[h][chunk] = zero

    def remote(src, dst, send, recv, device):
        return pltpu.make_async_remote_copy(
            src_ref=src, dst_ref=dst, send_sem=send, recv_sem=recv, device_id=device, device_id_type=MESH
        )

    def start_all(copies):
        for copy in copies:
            copy.start()

    def arrived(copies):
        for copy in copies:
            copy.wait_recv()

    def left(copies):
        for copy in copies:
            copy.wait_send()

    def products(h, base, pairs, lhs_ref, rhs_ref, unroll):
        def one(m, acc):
            a, b = base + 2 * m, base + 2 * m + 1
            lhs = jnp.concatenate([lhs_ref[h][idx[2 * pairs + a]], lhs_ref[h][idx[2 * pairs + b]]], axis=1)
            rhs = jnp.concatenate([rhs_ref[idx[a]], rhs_ref[idx[b]]], axis=0)
            acc = acc * idx[base + 4 * pairs + m].astype(F32)
            acc = acc + jnp.dot(lhs, rhs, preferred_element_type=F32)
            scan[h, m] = acc
            return acc

        def some(i, acc):
            for u in range(unroll):
                acc = one(i * unroll + u, acc)
            return acc

        lax.fori_loop(0, pairs // unroll, some, jnp.zeros(scan.shape[2:], F32))
        scan[h, pairs] = jnp.zeros(scan.shape[2:], F32)

    fwd_last = g["fwd_at"] + 5 * g["fwd_pairs"]
    adj_last = g["adj_at"] + 5 * g["adj_pairs"]
    gat_last = g["gat_at"] + 5 * g["gat_pairs"]

    def field_copies(h):
        own = ext[h].at[pl.ds(SIDE * chunk, chunk)]
        return [
            remote(own, ext[h].at[pl.ds((SIDE - d) * chunk, chunk)], es.at[h, i], er.at[h, i], holder(d))
            for i, d in enumerate(sides)
        ]

    def gather_copies(h):
        own = spread[h].at[pl.ds(c * chunk, chunk)]
        return [remote(own, own, gs.at[h, i], gr.at[h, i], obs_peer(r)) for i, r in enumerate(around)]

    def predicted_copies(h):
        copies = []
        for i, r in enumerate(far):
            peer = flux_peer(r)
            part = part_obs.at[h, pl.ds(peer[1] * mine, mine)]
            copies.append(remote(part, got_obs.at[h, i], fs.at[h, i], fr.at[h, i], peer))
        return copies

    def weighted_copies(h):
        own = weighted[h].at[pl.ds(f * mine, mine)]
        return [remote(own, own, ws.at[h, i], wr.at[h, i], flux_peer(r)) for i, r in enumerate(far)]

    def cell_copies(h):
        copies = []
        for i, r in enumerate(around):
            peer = obs_peer(r)
            part = part_cell.at[h, pl.ds(chunk_of(peer[0], f) * chunk, chunk)]
            copies.append(remote(part, got_cell.at[h, i], os_.at[h, i], or_.at[h, i], peer))
        return copies

    def contribution_copies(h):
        return [
            remote(
                part_field.at[h, pl.ds((SIDE + d) * chunk, chunk)], got_field.at[h, i],
                cs.at[h, i], cr.at[h, i], holder(d),
            )
            for i, d in enumerate(sides)
        ]

    def spread_phase(h, s):
        copies = field_copies(h)
        if h == 0:
            @pl.when(s == 0)
            def _():
                load_prior.wait()

        arrived(copies)
        for t in range(chunk):
            lhs = jnp.concatenate([ext[h][idx[g["nbr_at"] + t * nbrs + k]] for k in range(nbrs)], axis=1)
            rhs = prior_own[t].reshape(nbrs * prior_own.shape[2], prior_own.shape[3])
            spread[h][c * chunk + t] = jnp.dot(lhs, rhs, preferred_element_type=F32).astype(BF16)
        start_all(gather_copies(h))
        left(copies)

    def forward_phase(h, s):
        copies = gather_copies(h)
        if h == 0:
            @pl.when(s == 0)
            def _():
                for e in range(chunk * nbrs):
                    prior_flip[e] = prior_own[e // nbrs, e % nbrs].T
                load_jac.wait()

        arrived(copies)
        products(h, g["fwd_at"], g["fwd_pairs"], spread, blocks, g["fwd_unroll"])
        for b in range(obs_blocks):
            part_obs[h, b] = scan[h, idx[fwd_last + b]].astype(BF16)
        start_all(predicted_copies(h))
        left(copies)

    def weight_phase(h, s):
        copies = predicted_copies(h)
        if h == 0:
            @pl.when(s == 0)
            def _():
                many = unroll_of(slots, 8)

                def flip(i, carry):
                    for u in range(many):
                        flipped[i * many + u] = blocks[i * many + u].T
                    return carry

                lax.fori_loop(0, slots // many, flip, 0)

        arrived(copies)
        for b in range(mine):
            total = scan[h, idx[fwd_last + f * mine + b]]
            for i in range(len(far)):
                total = total + got_obs[h, i, b].astype(F32)
            weighted[h][f * mine + b] = (total * rinv[pl.ds(f * mine + b, 1), :]).astype(BF16)
        start_all(weighted_copies(h))
        left(copies)

    def adjoint_phase(h, s):
        copies = weighted_copies(h)
        arrived(copies)
        products(h, g["adj_at"], g["adj_pairs"], weighted, flipped, g["adj_unroll"])
        for t in range(tiles):
            part_cell[h, t] = scan[h, idx[adj_last + t]].astype(BF16)
        start_all(cell_copies(h))
        left(copies)

    def prior_phase(h, s):
        copies = cell_copies(h)
        arrived(copies)
        for t in range(chunk):
            total = scan[h, idx[adj_last + c * chunk + t]]
            for i in range(len(around)):
                total = total + got_cell[h, i, t].astype(F32)
            adjoint[h][t] = total.astype(BF16)
        products(h, g["gat_at"], g["gat_pairs"], adjoint, prior_flip, g["gat_unroll"])
        for j in range(reach):
            if j // chunk != SIDE:
                part_field[h, j] = scan[h, idx[gat_last + j]].astype(BF16)
        start_all(contribution_copies(h))
        left(copies)

    def field_phase(h, s):
        copies = contribution_copies(h)
        arrived(copies)
        for t in range(chunk):
            total = scan[h, idx[gat_last + SIDE * chunk + t]]
            for i in range(len(sides)):
                total = total + got_field[h, i, t].astype(F32)
            ext[h][SIDE * chunk + t] = total.astype(BF16)

        @pl.when(s < STEPS - 1)
        def _():
            start_all(field_copies(h))

        left(copies)

    for h in range(2):
        load_field[h].wait()
        start_all(field_copies(h))

    def step(s, carry):
        for phase in (spread_phase, forward_phase, weight_phase, adjoint_phase, prior_phase, field_phase):
            for h in range(2):
                phase(h, s)
        return carry

    lax.fori_loop(0, STEPS, step, 0)
    for h in range(2):
        for t in range(chunk):
            spread[h][c * chunk + t] = ext[h][SIDE * chunk + t]
        start_all(gather_copies(h))
    for h in range(2):
        copies = gather_copies(h)
        arrived(copies)
        left(copies)
        out[:, pl.ds(h * rows, rows), :] = spread[h][pl.ds(0, tiles)]


def shards(no, nf, flux_minor, probes, prior_tiles, neighbours, jac, jac_obs, jac_flux, counts, rinv):
    tiles, probe_count, width = probes.shape
    nbrs = prior_tiles.shape[1]
    obs_blocks = rinv.shape[0]
    slots = jac.shape[2]
    chunk = tiles // no
    assert SIDE * chunk == REACH and obs_blocks % nf == 0
    reach = (2 * SIDE + 1) * chunk
    fwd_pairs = (slots + obs_blocks) // 2
    adj_pairs = (slots + tiles) // 2
    gat_pairs = (chunk * nbrs + reach) // 2
    o = lax.axis_index("obs")
    f = lax.axis_index("flux")
    c = jnp.where(f % 2 == 1, no - 1 - o, o)
    live = jnp.arange(slots, dtype=jnp.int32) < counts[0, 0]
    block_obs, block_flux = jac_obs[0, 0], jac_flux[0, 0]
    own = lax.dynamic_slice_in_dim(neighbours, c * chunk, chunk, 0).reshape(-1)
    own = own - (f * tiles + c * chunk - SIDE * chunk)
    entry_tile = jnp.arange(chunk * nbrs, dtype=jnp.int32) // nbrs
    fwd = segment_pairs(jnp.where(live, block_obs, obs_blocks), block_flux, obs_blocks, tiles, fwd_pairs)
    adj = segment_pairs(jnp.where(live, block_flux, tiles), block_obs, tiles, obs_blocks, adj_pairs)
    gat = segment_pairs(own, entry_tile, reach, chunk, gat_pairs)
    idx = jnp.concatenate([fwd, adj, gat, own])
    g = dict(
        no=no, nf=nf, flux_minor=flux_minor, chunk=chunk, tiles=tiles, obs_blocks=obs_blocks, nbrs=nbrs, slots=slots,
        fwd_pairs=fwd_pairs, adj_pairs=adj_pairs, gat_pairs=gat_pairs,
        fwd_at=0, adj_at=fwd.shape[0], gat_at=fwd.shape[0] + adj.shape[0],
        nbr_at=fwd.shape[0] + adj.shape[0] + gat.shape[0],
        fwd_unroll=unroll_of(fwd_pairs, 108), adj_unroll=unroll_of(adj_pairs, 108),
        gat_unroll=unroll_of(gat_pairs, 56),
    )
    mine = obs_blocks // nf
    tile = (probe_count, width)
    half = (probe_count // 2, width)
    dma = pltpu.SemaphoreType.DMA
    most = max(fwd_pairs, adj_pairs, gat_pairs) + 1
    vmem = pl.BlockSpec(memory_space=pltpu.VMEM)
    any_space = pl.BlockSpec(memory_space=pl.ANY)
    return pl.pallas_call(
        functools.partial(kernel, g),
        out_shape=jax.ShapeDtypeStruct((tiles,) + tile, BF16),
        in_specs=[pl.BlockSpec(memory_space=pltpu.SMEM), any_space, any_space, any_space, vmem],
        out_specs=vmem,
        scratch_shapes=[
            pltpu.VMEM((slots, width, width), BF16),
            pltpu.VMEM((slots, width, width), BF16),
            pltpu.VMEM((chunk, nbrs, width, width), BF16),
            pltpu.VMEM((chunk * nbrs, width, width), BF16),
            pltpu.VMEM((reach,) + half, BF16), pltpu.VMEM((reach,) + half, BF16),
            pltpu.VMEM((tiles + 1,) + half, BF16), pltpu.VMEM((tiles + 1,) + half, BF16),
            pltpu.VMEM((obs_blocks + 1,) + half, BF16), pltpu.VMEM((obs_blocks + 1,) + half, BF16),
            pltpu.VMEM((chunk + 1,) + half, BF16), pltpu.VMEM((chunk + 1,) + half, BF16),
            pltpu.VMEM((2, most) + half, F32),
            pltpu.VMEM((2, obs_blocks) + half, BF16),
            pltpu.VMEM((2, nf - 1, mine) + half, BF16),
            pltpu.VMEM((2, tiles) + half, BF16),
            pltpu.VMEM((2, no - 1, chunk) + half, BF16),
            pltpu.VMEM((2, reach) + half, BF16),
            pltpu.VMEM((2, 2 * SIDE, chunk) + half, BF16),
            dma((4,)),
            dma((2, nf - 1)), dma((2, nf - 1)), dma((2, nf - 1)), dma((2, nf - 1)),
            dma((2, no - 1)), dma((2, no - 1)), dma((2, no - 1)), dma((2, no - 1)),
            dma((2, 2 * SIDE)), dma((2, 2 * SIDE)), dma((2, 2 * SIDE)), dma((2, 2 * SIDE)),
        ],
        compiler_params=pltpu.CompilerParams(
            collective_id=0, has_side_effects=True, vmem_limit_bytes=48 * 1024 * 1024
        ),
    )(idx, probes, prior_tiles, jac[0, 0], rinv)


def solution(mesh):
    placed = (
        P("flux", None, None),
        P("flux", None, None, None),
        P("flux", None),
        P("obs", "flux", None, None, None),
        P("obs", "flux", None),
        P("obs", "flux", None),
        P("obs", "flux"),
        P("obs", None),
    )
    return jax.shard_map(
        functools.partial(shards, mesh.shape["obs"], mesh.shape["flux"], FLUX_MINOR),
        mesh=mesh, in_specs=placed, out_specs=P("flux", None, None), check_vma=False,
    )
```

```python
import functools

import jax
import jax.numpy as jnp
from jax import lax
from jax.experimental import pallas as pl
from jax.experimental.pallas import tpu as pltpu
from jax.sharding import PartitionSpec as P

STEPS = 4
REACH = 12
FLUX_MINOR = 4
SIDE = 2
MESH = pl.DeviceIdType.MESH
F32 = jnp.float32
BF16 = jnp.bfloat16


def segment_pairs(key, lhs, segments, zero_lhs, pairs):
    count = key.shape[0]
    order = jnp.arange(count, dtype=jnp.int32)
    names = jnp.arange(segments, dtype=jnp.int32)
    hot = (key[:, None] == names[None, :]).astype(jnp.int32)
    size = jnp.sum(hot, axis=0)
    even = (size + 1) // 2 * 2
    begin = jnp.sum(jnp.where(names[None, :] < names[:, None], even[None, :], 0), axis=1)
    same = (key[None, :] == key[:, None]) & (order[None, :] < order[:, None])
    rank = jnp.sum(same.astype(jnp.int32), axis=1)
    place = jnp.where(key < segments, jnp.sum(hot * begin[None, :], axis=1) + rank, -1)
    slots = jnp.arange(2 * pairs, dtype=jnp.int32)
    match = slots[:, None] == place[None, :]
    block = jnp.sum(jnp.where(match, order[None, :], 0), axis=1)
    left = zero_lhs + jnp.sum(jnp.where(match, lhs[None, :] - zero_lhs, 0), axis=1)
    opens = (slots[::2][:, None] == begin[None, :]) & (size > 0)[None, :]
    flag = 1 - jnp.sum(opens.astype(jnp.int32), axis=1)
    last = jnp.where(size > 0, (begin + even) // 2 - 1, pairs)
    return jnp.concatenate([block, left, flag, last]).astype(jnp.int32)


def unroll_of(total, most):
    return max(u for u in range(1, most + 1) if total % u == 0)


def kernel(
    g, idx, probes, prior, jac, rinv, out,
    blocks, flipped, prior_own, prior_flip, ext_a, ext_b, spread_a, spread_b, weighted_a, weighted_b, adjoint_a, adjoint_b, scan,
    part_obs, got_obs, part_cell, got_cell, part_field, got_field,
    load_sem, fs, fr, ws, wr, os_, or_, gs, gr, cs, cr, es, er,
):
    no, nf, chunk = g["no"], g["nf"], g["chunk"]
    tiles, obs_blocks, nbrs, slots = g["tiles"], g["obs_blocks"], g["nbrs"], g["slots"]
    mine = obs_blocks // nf
    reach = (2 * SIDE + 1) * chunk
    ext, spread = (ext_a, ext_b), (spread_a, spread_b)
    weighted, adjoint = (weighted_a, weighted_b), (adjoint_a, adjoint_b)
    rows = ext_a.shape[1]
    o = lax.axis_index("obs")
    f = lax.axis_index("flux")
    chunks = no * nf

    def chunk_of(o_, f_):
        odd = lax.rem(f_, 2)
        return odd * (no - 1 - o_) + (1 - odd) * o_

    c = chunk_of(o, f)
    q = f * no + c

    def holder(distance):
        at = lax.rem(q + distance + chunks, chunks)
        f_ = lax.div(at, no)
        return (chunk_of(lax.rem(at, no), f_), f_)

    def flux_peer(r):
        y = g["flux_minor"]
        dz, dy = r
        z_ = lax.rem(lax.div(f, y) + dz, nf // y)
        y_ = lax.rem(lax.rem(f, y) + dy, y)
        return (o, z_ * y + y_)

    def obs_peer(r):
        return (lax.rem(o + r, no), f)

    def hops(d, n):
        return min(d, n - d)

    y = g["flux_minor"]
    far = [(dz, dy) for dz in range(nf // y) for dy in range(y) if dz + dy > 0]
    far.sort(key=lambda r: (-hops(r[0], nf // y) - hops(r[1], y), r))
    around = sorted(range(1, no), key=lambda r: (-hops(r, no), r))
    sides = [d for d in range(-SIDE, SIDE + 1) if d != 0]

    load_jac = pltpu.make_async_copy(jac, blocks, load_sem.at[0])
    load_prior = pltpu.make_async_copy(prior.at[pl.ds(c * chunk, chunk)], prior_own, load_sem.at[1])
    load_field = [
        pltpu.make_async_copy(
            probes.at[pl.ds(c * chunk, chunk), pl.ds(h * rows, rows)],
            ext[h].at[pl.ds(SIDE * chunk, chunk)], load_sem.at[2 + h],
        )
        for h in range(2)
    ]
    for copy in load_field:
        copy.start()
    load_prior.start()
    load_jac.start()

    barrier = pltpu.get_barrier_semaphore()
    partners = [flux_peer(r) for r in far] + [obs_peer(r) for r in around]
    partners += [holder(d) for d in sides]
    for partner in partners:
        pl.semaphore_signal(barrier, inc=1, device_id=partner, device_id_type=MESH)
    pl.semaphore_wait(barrier, len(partners))

    zero = jnp.zeros(spread_a.shape[1:], BF16)
    for h in range(2):
        spread[h][tiles] = zero
        weighted[h][obs_blocks] = zero
        adjoint[h][chunk] = zero

    def remote(src, dst, send, recv, device):
        return pltpu.make_async_remote_copy(
            src_ref=src, dst_ref=dst, send_sem=send, recv_sem=recv, device_id=device, device_id_type=MESH
        )

    def start_all(copies):
        for copy in copies:
            copy.start()

    def field_all(h):
        return remote(*[ext[h].at[pl.ds(0, len(sides) * chunk)]] * 2, es.at[h], er.at[h], holder(1))

    def gather_all(h):
        return remote(*[spread[h].at[pl.ds(0, len(around) * chunk)]] * 2, gs.at[h], gr.at[h], obs_peer(1))

    def predicted_all(h):
        return remote(got_obs.at[h], got_obs.at[h], fs.at[h], fr.at[h], obs_peer(1))

    def weighted_all(h):
        return remote(*[weighted[h].at[pl.ds(0, len(far) * mine)]] * 2, ws.at[h], wr.at[h], obs_peer(1))

    def cell_all(h):
        return remote(got_cell.at[h], got_cell.at[h], os_.at[h], or_.at[h], obs_peer(1))

    def contribution_all(h):
        return remote(got_field.at[h], got_field.at[h], cs.at[h], cr.at[h], obs_peer(1))

    def products(h, base, pairs, lhs_ref, rhs_ref, unroll):
        def one(m, acc):
            a, b = base + 2 * m, base + 2 * m + 1
            lhs = jnp.concatenate([lhs_ref[h][idx[2 * pairs + a]], lhs_ref[h][idx[2 * pairs + b]]], axis=1)
            rhs = jnp.concatenate([rhs_ref[idx[a]], rhs_ref[idx[b]]], axis=0)
            acc = acc * idx[base + 4 * pairs + m].astype(F32)
            acc = acc + jnp.dot(lhs, rhs, preferred_element_type=F32)
            scan[h, m] = acc
            return acc

        def some(i, acc):
            for u in range(unroll):
                acc = one(i * unroll + u, acc)
            return acc

        lax.fori_loop(0, pairs // unroll, some, jnp.zeros(scan.shape[2:], F32))
        scan[h, pairs] = jnp.zeros(scan.shape[2:], F32)

    fwd_last = g["fwd_at"] + 5 * g["fwd_pairs"]
    adj_last = g["adj_at"] + 5 * g["adj_pairs"]
    gat_last = g["gat_at"] + 5 * g["gat_pairs"]

    def field_copies(h):
        own = ext[h].at[pl.ds(SIDE * chunk, chunk)]
        return [
            remote(own, ext[h].at[pl.ds((SIDE - d) * chunk, chunk)], es.at[h], er.at[h], holder(d))
            for i, d in enumerate(sides)
        ]

    def gather_copies(h):
        own = spread[h].at[pl.ds(c * chunk, chunk)]
        return [remote(own, own, gs.at[h], gr.at[h], obs_peer(r)) for i, r in enumerate(around)]

    def predicted_copies(h):
        copies = []
        for i, r in enumerate(far):
            peer = flux_peer(r)
            part = part_obs.at[h, pl.ds(peer[1] * mine, mine)]
            copies.append(remote(part, got_obs.at[h, i], fs.at[h], fr.at[h], peer))
        return copies

    def weighted_copies(h):
        own = weighted[h].at[pl.ds(f * mine, mine)]
        return [remote(own, own, ws.at[h], wr.at[h], flux_peer(r)) for i, r in enumerate(far)]

    def cell_copies(h):
        copies = []
        for i, r in enumerate(around):
            peer = obs_peer(r)
            part = part_cell.at[h, pl.ds(chunk_of(peer[0], f) * chunk, chunk)]
            copies.append(remote(part, got_cell.at[h, i], os_.at[h], or_.at[h], peer))
        return copies

    def contribution_copies(h):
        return [
            remote(
                part_field.at[h, pl.ds((SIDE + d) * chunk, chunk)], got_field.at[h, i],
                cs.at[h], cr.at[h], holder(d),
            )
            for i, d in enumerate(sides)
        ]

    def spread_phase(h, s):
        every = field_all(h)
        if h == 0:
            @pl.when(s == 0)
            def _():
                load_prior.wait()

        every.wait_recv()
        for t in range(chunk):
            lhs = jnp.concatenate([ext[h][idx[g["nbr_at"] + t * nbrs + k]] for k in range(nbrs)], axis=1)
            rhs = prior_own[t].reshape(nbrs * prior_own.shape[2], prior_own.shape[3])
            spread[h][c * chunk + t] = jnp.dot(lhs, rhs, preferred_element_type=F32).astype(BF16)
        start_all(gather_copies(h))
        every.wait_send()

    def forward_phase(h, s):
        every = gather_all(h)
        if h == 0:
            @pl.when(s == 0)
            def _():
                for e in range(chunk * nbrs):
                    prior_flip[e] = prior_own[e // nbrs, e % nbrs].T
                load_jac.wait()

        every.wait_recv()
        products(h, g["fwd_at"], g["fwd_pairs"], spread, blocks, g["fwd_unroll"])
        for b in range(obs_blocks):
            part_obs[h, b] = scan[h, idx[fwd_last + b]].astype(BF16)
        start_all(predicted_copies(h))
        every.wait_send()

    def weight_phase(h, s):
        every = predicted_all(h)
        if h == 0:
            @pl.when(s == 0)
            def _():
                many = unroll_of(slots, 8)

                def flip(i, carry):
                    for u in range(many):
                        flipped[i * many + u] = blocks[i * many + u].T
                    return carry

                lax.fori_loop(0, slots // many, flip, 0)

        every.wait_recv()
        for b in range(mine):
            total = scan[h, idx[fwd_last + f * mine + b]]
            for i in range(len(far)):
                total = total + got_obs[h, i, b].astype(F32)
            weighted[h][f * mine + b] = (total * rinv[pl.ds(f * mine + b, 1), :]).astype(BF16)
        start_all(weighted_copies(h))
        every.wait_send()

    def adjoint_phase(h, s):
        every = weighted_all(h)
        every.wait_recv()
        products(h, g["adj_at"], g["adj_pairs"], weighted, flipped, g["adj_unroll"])
        for t in range(tiles):
            part_cell[h, t] = scan[h, idx[adj_last + t]].astype(BF16)
        start_all(cell_copies(h))
        every.wait_send()

    def prior_phase(h, s):
        every = cell_all(h)
        every.wait_recv()
        for t in range(chunk):
            total = scan[h, idx[adj_last + c * chunk + t]]
            for i in range(len(around)):
                total = total + got_cell[h, i, t].astype(F32)
            adjoint[h][t] = total.astype(BF16)
        products(h, g["gat_at"], g["gat_pairs"], adjoint, prior_flip, g["gat_unroll"])
        for j in range(reach):
            if j // chunk != SIDE:
                part_field[h, j] = scan[h, idx[gat_last + j]].astype(BF16)
        start_all(contribution_copies(h))
        every.wait_send()

    def field_phase(h, s):
        every = contribution_all(h)
        every.wait_recv()
        for t in range(chunk):
            total = scan[h, idx[gat_last + SIDE * chunk + t]]
            for i in range(len(sides)):
                total = total + got_field[h, i, t].astype(F32)
            ext[h][SIDE * chunk + t] = total.astype(BF16)

        @pl.when(s < STEPS - 1)
        def _():
            start_all(field_copies(h))

        every.wait_send()

    for h in range(2):
        load_field[h].wait()
        start_all(field_copies(h))

    def step(s, carry):
        for phase in (spread_phase, forward_phase, weight_phase, adjoint_phase, prior_phase, field_phase):
            for h in range(2):
                phase(h, s)
        return carry

    lax.fori_loop(0, STEPS, step, 0)
    for h in range(2):
        for t in range(chunk):
            spread[h][c * chunk + t] = ext[h][SIDE * chunk + t]
        start_all(gather_copies(h))
    for h in range(2):
        every = gather_all(h)
        every.wait_recv()
        every.wait_send()
        out[:, pl.ds(h * rows, rows), :] = spread[h][pl.ds(0, tiles)]


def shards(no, nf, flux_minor, probes, prior_tiles, neighbours, jac, jac_obs, jac_flux, counts, rinv):
    tiles, probe_count, width = probes.shape
    nbrs = prior_tiles.shape[1]
    obs_blocks = rinv.shape[0]
    slots = jac.shape[2]
    chunk = tiles // no
    assert SIDE * chunk == REACH and obs_blocks % nf == 0
    reach = (2 * SIDE + 1) * chunk
    fwd_pairs = (slots + obs_blocks) // 2
    adj_pairs = (slots + tiles) // 2
    gat_pairs = (chunk * nbrs + reach) // 2
    o = lax.axis_index("obs")
    f = lax.axis_index("flux")
    c = jnp.where(f % 2 == 1, no - 1 - o, o)
    live = jnp.arange(slots, dtype=jnp.int32) < counts[0, 0]
    block_obs, block_flux = jac_obs[0, 0], jac_flux[0, 0]
    own = lax.dynamic_slice_in_dim(neighbours, c * chunk, chunk, 0).reshape(-1)
    own = own - (f * tiles + c * chunk - SIDE * chunk)
    entry_tile = jnp.arange(chunk * nbrs, dtype=jnp.int32) // nbrs
    fwd = segment_pairs(jnp.where(live, block_obs, obs_blocks), block_flux, obs_blocks, tiles, fwd_pairs)
    adj = segment_pairs(jnp.where(live, block_flux, tiles), block_obs, tiles, obs_blocks, adj_pairs)
    gat = segment_pairs(own, entry_tile, reach, chunk, gat_pairs)
    idx = jnp.concatenate([fwd, adj, gat, own])
    g = dict(
        no=no, nf=nf, flux_minor=flux_minor, chunk=chunk, tiles=tiles, obs_blocks=obs_blocks, nbrs=nbrs, slots=slots,
        fwd_pairs=fwd_pairs, adj_pairs=adj_pairs, gat_pairs=gat_pairs,
        fwd_at=0, adj_at=fwd.shape[0], gat_at=fwd.shape[0] + adj.shape[0],
        nbr_at=fwd.shape[0] + adj.shape[0] + gat.shape[0],
        fwd_unroll=unroll_of(fwd_pairs, 108), adj_unroll=unroll_of(adj_pairs, 108),
        gat_unroll=unroll_of(gat_pairs, 56),
    )
    mine = obs_blocks // nf
    tile = (probe_count, width)
    half = (probe_count // 2, width)
    dma = pltpu.SemaphoreType.DMA
    most = max(fwd_pairs, adj_pairs, gat_pairs) + 1
    vmem = pl.BlockSpec(memory_space=pltpu.VMEM)
    any_space = pl.BlockSpec(memory_space=pl.ANY)
    return pl.pallas_call(
        functools.partial(kernel, g),
        out_shape=jax.ShapeDtypeStruct((tiles,) + tile, BF16),
        in_specs=[pl.BlockSpec(memory_space=pltpu.SMEM), any_space, any_space, any_space, vmem],
        out_specs=vmem,
        scratch_shapes=[
            pltpu.VMEM((slots, width, width), BF16),
            pltpu.VMEM((slots, width, width), BF16),
            pltpu.VMEM((chunk, nbrs, width, width), BF16),
            pltpu.VMEM((chunk * nbrs, width, width), BF16),
            pltpu.VMEM((reach,) + half, BF16), pltpu.VMEM((reach,) + half, BF16),
            pltpu.VMEM((tiles + 1,) + half, BF16), pltpu.VMEM((tiles + 1,) + half, BF16),
            pltpu.VMEM((obs_blocks + 1,) + half, BF16), pltpu.VMEM((obs_blocks + 1,) + half, BF16),
            pltpu.VMEM((chunk + 1,) + half, BF16), pltpu.VMEM((chunk + 1,) + half, BF16),
            pltpu.VMEM((2, most) + half, F32),
            pltpu.VMEM((2, obs_blocks) + half, BF16),
            pltpu.VMEM((2, nf - 1, mine) + half, BF16),
            pltpu.VMEM((2, tiles) + half, BF16),
            pltpu.VMEM((2, no - 1, chunk) + half, BF16),
            pltpu.VMEM((2, reach) + half, BF16),
            pltpu.VMEM((2, 2 * SIDE, chunk) + half, BF16),
            dma((4,)),
            dma((2,)), dma((2,)), dma((2,)), dma((2,)),
            dma((2,)), dma((2,)), dma((2,)), dma((2,)),
            dma((2,)), dma((2,)), dma((2,)), dma((2,)),
        ],
        compiler_params=pltpu.CompilerParams(
            collective_id=0, has_side_effects=True, vmem_limit_bytes=48 * 1024 * 1024
        ),
    )(idx, probes, prior_tiles, jac[0, 0], rinv)


def solution(mesh):
    placed = (
        P("flux", None, None),
        P("flux", None, None, None),
        P("flux", None),
        P("obs", "flux", None, None, None),
        P("obs", "flux", None),
        P("obs", "flux", None),
        P("obs", "flux"),
        P("obs", None),
    )
    return jax.shard_map(
        functools.partial(shards, mesh.shape["obs"], mesh.shape["flux"], FLUX_MINOR),
        mesh=mesh, in_specs=placed, out_specs=P("flux", None, None), check_vma=False,
    )
```

```python
import functools

import jax
import jax.numpy as jnp
from jax import lax
from jax.experimental import pallas as pl
from jax.experimental.pallas import tpu as pltpu
from jax.sharding import PartitionSpec as P

STEPS = 4
REACH = 12
FLUX_MINOR = 4
SIDE = 2
MESH = pl.DeviceIdType.MESH
F32 = jnp.float32
BF16 = jnp.bfloat16


LANES = 128
NOBODY = LANES - 1


def iota(shape, dim):
    return lax.broadcasted_iota(jnp.int32, shape, dim)


def column(row):
    parts = [
        jnp.broadcast_to(row[:, i : i + LANES], (LANES, LANES)).T for i in range(0, row.shape[1], LANES)
    ]
    return jnp.concatenate(parts, axis=0) if len(parts) > 1 else parts[0]


def total(values):
    return jnp.sum(values, axis=0, keepdims=True)


def segment_pairs(table, at, key, lhs, zero_lhs, pairs):
    count = key.shape[1]
    square = (LANES, LANES)
    key_col = column(key)
    size = total((key_col == iota((count, LANES), 1)).astype(jnp.int32))
    even = ((size + 1) >> 1) << 1
    begin = total(jnp.where(iota(square, 0) < iota(square, 1), column(even), 0))
    begin_col, size_col = column(begin), column(size)
    place = []
    for i in range(0, count, LANES):
        here = key[:, i : i + LANES]
        first = total(jnp.where(iota(square, 0) == here, begin_col, 0))
        same = (key_col == here) & (iota((count, LANES), 0) < iota((count, LANES), 1) + i)
        place.append(first + total(same.astype(jnp.int32)))
    place_col = column(jnp.concatenate(place, axis=1) if len(place) > 1 else place[0])
    packed = jnp.where(key_col == NOBODY, 0, (column(lhs) + 1) * 1024 + iota((count, LANES), 0))
    for i in range(0, 2 * pairs, LANES):
        found = total(jnp.where(place_col == iota((count, LANES), 1) + i, packed, 0))
        table[at : at + 1, i : i + LANES] = found & 1023
        table[at + 1 : at + 2, i : i + LANES] = jnp.where(found == 0, zero_lhs, (found >> 10) - 1)
    for i in range(0, 2 * LANES, LANES):
        opens = (begin_col == 2 * (iota(square, 1) + i)) & (size_col > 0)
        table[at + 2 : at + 3, i : i + LANES] = 1 - total(opens.astype(jnp.int32))
    table[at + 2 : at + 3, 2 * LANES : 3 * LANES] = jnp.where(size > 0, ((begin + even) >> 1) - 1, pairs)


def unroll_of(total, most):
    return max(u for u in range(1, most + 1) if total % u == 0)


def kernel(
    g, near_in, obs_in, cell_in, counts_in, probes, prior, jac, rinv_in, out,
    idx, table, near, obs_row, cell_row, count, rinv,
    blocks, flipped, prior_own, prior_flip, ext_a, ext_b, spread_a, spread_b, weighted_a, weighted_b, adjoint_a, adjoint_b, scan,
    part_obs, got_obs, part_cell, got_cell, part_field, got_field,
    load_sem, fs, fr, ws, wr, os_, or_, gs, gr, cs, cr, es, er,
):
    no, nf, chunk = g["no"], g["nf"], g["chunk"]
    tiles, obs_blocks, nbrs, slots = g["tiles"], g["obs_blocks"], g["nbrs"], g["slots"]
    mine = obs_blocks // nf
    reach = (2 * SIDE + 1) * chunk
    ext, spread = (ext_a, ext_b), (spread_a, spread_b)
    weighted, adjoint = (weighted_a, weighted_b), (adjoint_a, adjoint_b)
    rows = ext_a.shape[1]
    o = lax.axis_index("obs")
    f = lax.axis_index("flux")
    chunks = no * nf

    def chunk_of(o_, f_):
        odd = lax.rem(f_, 2)
        return odd * (no - 1 - o_) + (1 - odd) * o_

    c = chunk_of(o, f)
    q = f * no + c

    def holder(distance):
        at = lax.rem(q + distance + chunks, chunks)
        f_ = lax.div(at, no)
        return (chunk_of(lax.rem(at, no), f_), f_)

    def flux_peer(r):
        y = g["flux_minor"]
        dz, dy = r
        z_ = lax.rem(lax.div(f, y) + dz, nf // y)
        y_ = lax.rem(lax.rem(f, y) + dy, y)
        return (o, z_ * y + y_)

    def obs_peer(r):
        return (lax.rem(o + r, no), f)

    def hops(d, n):
        return min(d, n - d)

    y = g["flux_minor"]
    far = [(dz, dy) for dz in range(nf // y) for dy in range(y) if dz + dy > 0]
    far.sort(key=lambda r: (-hops(r[0], nf // y) - hops(r[1], y), r))
    around = sorted(range(1, no), key=lambda r: (-hops(r, no), r))
    sides = [d for d in range(-SIDE, SIDE + 1) if d != 0]

    load_jac = pltpu.make_async_copy(jac, blocks, load_sem.at[0])
    load_prior = pltpu.make_async_copy(prior.at[pl.ds(c * chunk, chunk)], prior_own, load_sem.at[1])
    load_field = [
        pltpu.make_async_copy(
            probes.at[pl.ds(c * chunk, chunk), pl.ds(h * rows, rows)],
            ext[h].at[pl.ds(SIDE * chunk, chunk)], load_sem.at[2 + h],
        )
        for h in range(2)
    ]
    small = [(near_in, near), (obs_in, obs_row), (cell_in, cell_row), (counts_in, count), (rinv_in, rinv)]
    load_small = [pltpu.make_async_copy(a, b, load_sem.at[5 + i]) for i, (a, b) in enumerate(small)]
    for copy in load_small + load_field:
        copy.start()
    load_prior.start()
    load_jac.start()

    barrier = pltpu.get_barrier_semaphore()
    partners = [flux_peer(r) for r in far] + [obs_peer(r) for r in around]
    partners += [holder(d) for d in sides]
    for partner in partners:
        pl.semaphore_signal(barrier, inc=1, device_id=partner, device_id_type=MESH)

    for copy in load_small:
        copy.wait()
    live = iota((1, slots), 1) < jnp.broadcast_to(count[...], (1, slots))
    by_obs, by_cell = obs_row[0], cell_row[0]
    segment_pairs(table, 0, jnp.where(live, by_obs, NOBODY), by_cell, tiles, g["fwd_pairs"])
    segment_pairs(table, 3, jnp.where(live, by_cell, NOBODY), by_obs, obs_blocks, g["adj_pairs"])
    entry = iota((1, LANES), 1)
    by_near = jnp.where(entry < chunk * nbrs, near[...], NOBODY)
    segment_pairs(table, 6, by_near, jnp.minimum(entry // nbrs, chunk - 1), chunk, g["gat_pairs"])
    table[9:10, :LANES] = near[...]
    load_index = pltpu.make_async_copy(table, idx, load_sem.at[4])
    load_index.start()
    pl.semaphore_wait(barrier, len(partners))

    zero = jnp.zeros(spread_a.shape[1:], BF16)
    for h in range(2):
        spread[h][tiles] = zero
        weighted[h][obs_blocks] = zero
        adjoint[h][chunk] = zero

    def remote(src, dst, send, recv, device):
        return pltpu.make_async_remote_copy(
            src_ref=src, dst_ref=dst, send_sem=send, recv_sem=recv, device_id=device, device_id_type=MESH
        )

    def start_all(copies):
        for copy in copies:
            copy.start()

    def field_all(h):
        return remote(*[ext[h].at[pl.ds(0, len(sides) * chunk)]] * 2, es.at[h], er.at[h], holder(1))

    def gather_all(h):
        return remote(*[spread[h].at[pl.ds(0, len(around) * chunk)]] * 2, gs.at[h], gr.at[h], obs_peer(1))

    def predicted_all(h):
        return remote(got_obs.at[h], got_obs.at[h], fs.at[h], fr.at[h], obs_peer(1))

    def weighted_all(h):
        return remote(*[weighted[h].at[pl.ds(0, len(far) * mine)]] * 2, ws.at[h], wr.at[h], obs_peer(1))

    def cell_all(h):
        return remote(got_cell.at[h], got_cell.at[h], os_.at[h], or_.at[h], obs_peer(1))

    def contribution_all(h):
        return remote(got_field.at[h], got_field.at[h], cs.at[h], cr.at[h], obs_peer(1))

    def products(h, base, pairs, lhs_ref, rhs_ref, unroll):
        def one(m, acc):
            a, b = 2 * m, 2 * m + 1
            lhs = jnp.concatenate([lhs_ref[h][idx[base + 1, a]], lhs_ref[h][idx[base + 1, b]]], axis=1)
            rhs = jnp.concatenate([rhs_ref[idx[base, a]], rhs_ref[idx[base, b]]], axis=0)
            acc = acc * idx[base + 2, m].astype(F32)
            acc = acc + jnp.dot(lhs, rhs, preferred_element_type=F32)
            scan[h, m] = acc
            return acc

        def some(i, acc):
            for u in range(unroll):
                acc = one(i * unroll + u, acc)
            return acc

        lax.fori_loop(0, pairs // unroll, some, jnp.zeros(scan.shape[2:], F32))
        scan[h, pairs] = jnp.zeros(scan.shape[2:], F32)

    def last_of(base, segment):
        return idx[base + 2, 2 * LANES + segment]

    def field_copies(h):
        own = ext[h].at[pl.ds(SIDE * chunk, chunk)]
        return [
            remote(own, ext[h].at[pl.ds((SIDE - d) * chunk, chunk)], es.at[h], er.at[h], holder(d))
            for i, d in enumerate(sides)
        ]

    def gather_copies(h):
        own = spread[h].at[pl.ds(c * chunk, chunk)]
        return [remote(own, own, gs.at[h], gr.at[h], obs_peer(r)) for i, r in enumerate(around)]

    def predicted_copies(h):
        copies = []
        for i, r in enumerate(far):
            peer = flux_peer(r)
            part = part_obs.at[h, pl.ds(peer[1] * mine, mine)]
            copies.append(remote(part, got_obs.at[h, i], fs.at[h], fr.at[h], peer))
        return copies

    def weighted_copies(h):
        own = weighted[h].at[pl.ds(f * mine, mine)]
        return [remote(own, own, ws.at[h], wr.at[h], flux_peer(r)) for i, r in enumerate(far)]

    def cell_copies(h):
        copies = []
        for i, r in enumerate(around):
            peer = obs_peer(r)
            part = part_cell.at[h, pl.ds(chunk_of(peer[0], f) * chunk, chunk)]
            copies.append(remote(part, got_cell.at[h, i], os_.at[h], or_.at[h], peer))
        return copies

    def contribution_copies(h):
        return [
            remote(
                part_field.at[h, pl.ds((SIDE + d) * chunk, chunk)], got_field.at[h, i],
                cs.at[h], cr.at[h], holder(d),
            )
            for i, d in enumerate(sides)
        ]

    def spread_phase(h, s):
        every = field_all(h)
        if h == 0:
            @pl.when(s == 0)
            def _():
                load_index.wait()
                load_prior.wait()

        every.wait_recv()
        for t in range(chunk):
            lhs = jnp.concatenate([ext[h][idx[9, t * nbrs + k]] for k in range(nbrs)], axis=1)
            rhs = prior_own[t].reshape(nbrs * prior_own.shape[2], prior_own.shape[3])
            spread[h][c * chunk + t] = jnp.dot(lhs, rhs, preferred_element_type=F32).astype(BF16)
        start_all(gather_copies(h))
        every.wait_send()

    def forward_phase(h, s):
        every = gather_all(h)
        if h == 0:
            @pl.when(s == 0)
            def _():
                for e in range(chunk * nbrs):
                    prior_flip[e] = prior_own[e // nbrs, e % nbrs].T
                load_jac.wait()

        every.wait_recv()
        products(h, 0, g["fwd_pairs"], spread, blocks, g["fwd_unroll"])
        for b in range(obs_blocks):
            part_obs[h, b] = scan[h, last_of(0, b)].astype(BF16)
        start_all(predicted_copies(h))
        every.wait_send()

    def weight_phase(h, s):
        every = predicted_all(h)
        if h == 0:
            @pl.when(s == 0)
            def _():
                many = unroll_of(slots, 8)

                def flip(i, carry):
                    for u in range(many):
                        flipped[i * many + u] = blocks[i * many + u].T
                    return carry

                lax.fori_loop(0, slots // many, flip, 0)

        every.wait_recv()
        for b in range(mine):
            value = scan[h, last_of(0, f * mine + b)]
            for i in range(len(far)):
                value = value + got_obs[h, i, b].astype(F32)
            weighted[h][f * mine + b] = (value * rinv[pl.ds(f * mine + b, 1), :]).astype(BF16)
        start_all(weighted_copies(h))
        every.wait_send()

    def adjoint_phase(h, s):
        every = weighted_all(h)
        every.wait_recv()
        products(h, 3, g["adj_pairs"], weighted, flipped, g["adj_unroll"])
        for t in range(tiles):
            part_cell[h, t] = scan[h, last_of(3, t)].astype(BF16)
        start_all(cell_copies(h))
        every.wait_send()

    def prior_phase(h, s):
        every = cell_all(h)
        every.wait_recv()
        for t in range(chunk):
            value = scan[h, last_of(3, c * chunk + t)]
            for i in range(len(around)):
                value = value + got_cell[h, i, t].astype(F32)
            adjoint[h][t] = value.astype(BF16)
        products(h, 6, g["gat_pairs"], adjoint, prior_flip, g["gat_unroll"])
        for j in range(reach):
            if j // chunk != SIDE:
                part_field[h, j] = scan[h, last_of(6, j)].astype(BF16)
        start_all(contribution_copies(h))
        every.wait_send()

    def field_phase(h, s):
        every = contribution_all(h)
        every.wait_recv()
        for t in range(chunk):
            value = scan[h, last_of(6, SIDE * chunk + t)]
            for i in range(len(sides)):
                value = value + got_field[h, i, t].astype(F32)
            ext[h][SIDE * chunk + t] = value.astype(BF16)

        @pl.when(s < STEPS - 1)
        def _():
            start_all(field_copies(h))

        every.wait_send()

    for h in range(2):
        load_field[h].wait()
        start_all(field_copies(h))

    def step(s, carry):
        for phase in (spread_phase, forward_phase, weight_phase, adjoint_phase, prior_phase, field_phase):
            for h in range(2):
                phase(h, s)
        return carry

    lax.fori_loop(0, STEPS, step, 0)
    for h in range(2):
        for t in range(chunk):
            spread[h][c * chunk + t] = ext[h][SIDE * chunk + t]
        start_all(gather_copies(h))
    for h in range(2):
        every = gather_all(h)
        every.wait_recv()
        every.wait_send()
        out[:, pl.ds(h * rows, rows), :] = spread[h][pl.ds(0, tiles)]


def shards(no, nf, flux_minor, probes, prior_tiles, neighbours, jac, jac_obs, jac_flux, counts, rinv):
    tiles, probe_count, width = probes.shape
    nbrs = prior_tiles.shape[1]
    obs_blocks = rinv.shape[0]
    slots = jac.shape[2]
    chunk = tiles // no
    assert SIDE * chunk == REACH and obs_blocks % nf == 0
    reach = (2 * SIDE + 1) * chunk
    fwd_pairs = (slots + obs_blocks) // 2
    adj_pairs = (slots + tiles) // 2
    gat_pairs = (chunk * nbrs + reach) // 2
    o = lax.axis_index("obs")
    f = lax.axis_index("flux")
    c = jnp.where(f % 2 == 1, no - 1 - o, o)
    own = lax.dynamic_slice_in_dim(neighbours, c * chunk, chunk, 0).reshape(1, -1)
    own = own - (f * tiles + c * chunk - SIDE * chunk)
    own = jnp.pad(own, ((0, 0), (0, LANES - own.shape[1])), constant_values=NOBODY)
    assert slots % LANES == 0 and slots < 1024 and max(reach, tiles, obs_blocks) < NOBODY
    assert max(fwd_pairs, adj_pairs) <= 2 * LANES and chunk * nbrs <= LANES
    g = dict(
        no=no, nf=nf, flux_minor=flux_minor, chunk=chunk, tiles=tiles, obs_blocks=obs_blocks, nbrs=nbrs, slots=slots,
        fwd_pairs=fwd_pairs, adj_pairs=adj_pairs, gat_pairs=gat_pairs,
        fwd_unroll=unroll_of(fwd_pairs, 108), adj_unroll=unroll_of(adj_pairs, 108),
        gat_unroll=unroll_of(gat_pairs, 56),
    )
    mine = obs_blocks // nf
    tile = (probe_count, width)
    half = (probe_count // 2, width)
    dma = pltpu.SemaphoreType.DMA
    most = max(fwd_pairs, adj_pairs, gat_pairs) + 1
    vmem = pl.BlockSpec(memory_space=pltpu.VMEM)
    any_space = pl.BlockSpec(memory_space=pl.ANY)
    return pl.pallas_call(
        functools.partial(kernel, g),
        out_shape=jax.ShapeDtypeStruct((tiles,) + tile, BF16),
        in_specs=[any_space] * 8,
        out_specs=vmem,
        scratch_shapes=[
            pltpu.SMEM((16, 4 * LANES), jnp.int32),
            pltpu.VMEM((16, 4 * LANES), jnp.int32),
            pltpu.VMEM((1, LANES), jnp.int32),
            pltpu.VMEM((1, 1, slots), jnp.int32),
            pltpu.VMEM((1, 1, slots), jnp.int32),
            pltpu.VMEM((1, 1), jnp.int32),
            pltpu.VMEM((obs_blocks, width), F32),
            pltpu.VMEM((slots, width, width), BF16),
            pltpu.VMEM((slots, width, width), BF16),
            pltpu.VMEM((chunk, nbrs, width, width), BF16),
            pltpu.VMEM((chunk * nbrs, width, width), BF16),
            pltpu.VMEM((reach,) + half, BF16), pltpu.VMEM((reach,) + half, BF16),
            pltpu.VMEM((tiles + 1,) + half, BF16), pltpu.VMEM((tiles + 1,) + half, BF16),
            pltpu.VMEM((obs_blocks + 1,) + half, BF16), pltpu.VMEM((obs_blocks + 1,) + half, BF16),
            pltpu.VMEM((chunk + 1,) + half, BF16), pltpu.VMEM((chunk + 1,) + half, BF16),
            pltpu.VMEM((2, most) + half, F32),
            pltpu.VMEM((2, obs_blocks) + half, BF16),
            pltpu.VMEM((2, nf - 1, mine) + half, BF16),
            pltpu.VMEM((2, tiles) + half, BF16),
            pltpu.VMEM((2, no - 1, chunk) + half, BF16),
            pltpu.VMEM((2, reach) + half, BF16),
            pltpu.VMEM((2, 2 * SIDE, chunk) + half, BF16),
            dma((10,)),
            dma((2,)), dma((2,)), dma((2,)), dma((2,)),
            dma((2,)), dma((2,)), dma((2,)), dma((2,)),
            dma((2,)), dma((2,)), dma((2,)), dma((2,)),
        ],
        compiler_params=pltpu.CompilerParams(
            collective_id=0, has_side_effects=True, vmem_limit_bytes=48 * 1024 * 1024
        ),
    )(own, jac_obs, jac_flux, counts, probes, prior_tiles, jac[0, 0], rinv)


def solution(mesh):
    placed = (
        P("flux", None, None),
        P("flux", None, None, None),
        P("flux", None),
        P("obs", "flux", None, None, None),
        P("obs", "flux", None),
        P("obs", "flux", None),
        P("obs", "flux"),
        P("obs", None),
    )
    return jax.shard_map(
        functools.partial(shards, mesh.shape["obs"], mesh.shape["flux"], FLUX_MINOR),
        mesh=mesh, in_specs=placed, out_specs=P("flux", None, None), check_vma=False,
    )
```

```python
import functools

import jax
import jax.numpy as jnp
from jax import lax
from jax.experimental import pallas as pl
from jax.experimental.pallas import tpu as pltpu
from jax.sharding import PartitionSpec as P

STEPS = 4
REACH = 12
FLUX_MINOR = 4
SIDE = 2
MESH = pl.DeviceIdType.MESH
F32 = jnp.float32
BF16 = jnp.bfloat16


LANES = 128
NOBODY = LANES - 1


def iota(shape, dim):
    return lax.broadcasted_iota(jnp.int32, shape, dim)


def column(row):
    parts = [
        jnp.broadcast_to(row[:, i : i + LANES], (LANES, LANES)).T for i in range(0, row.shape[1], LANES)
    ]
    return jnp.concatenate(parts, axis=0) if len(parts) > 1 else parts[0]


def total(values):
    return jnp.sum(values, axis=0, keepdims=True)


def segment_pairs(table, at, key, lhs, zero_lhs, pairs):
    count = key.shape[1]
    square = (LANES, LANES)
    key_col = column(key)
    size = total((key_col == iota((count, LANES), 1)).astype(jnp.int32))
    even = ((size + 1) >> 1) << 1
    begin = total(jnp.where(iota(square, 0) < iota(square, 1), column(even), 0))
    begin_col, size_col = column(begin), column(size)
    place = []
    for i in range(0, count, LANES):
        here = key[:, i : i + LANES]
        first = total(jnp.where(iota(square, 0) == here, begin_col, 0))
        same = (key_col == here) & (iota((count, LANES), 0) < iota((count, LANES), 1) + i)
        place.append(first + total(same.astype(jnp.int32)))
    place_col = column(jnp.concatenate(place, axis=1) if len(place) > 1 else place[0])
    packed = jnp.where(key_col == NOBODY, 0, (column(lhs) + 1) * 1024 + iota((count, LANES), 0))
    for i in range(0, 2 * pairs, LANES):
        found = total(jnp.where(place_col == iota((count, LANES), 1) + i, packed, 0))
        table[at : at + 1, i : i + LANES] = found & 1023
        table[at + 1 : at + 2, i : i + LANES] = jnp.where(found == 0, zero_lhs, (found >> 10) - 1)
    for i in range(0, 2 * LANES, LANES):
        opens = (begin_col == 2 * (iota(square, 1) + i)) & (size_col > 0)
        table[at + 2 : at + 3, i : i + LANES] = 1 - total(opens.astype(jnp.int32))
    table[at + 2 : at + 3, 2 * LANES : 3 * LANES] = jnp.where(size > 0, ((begin + even) >> 1) - 1, pairs)


def unroll_of(total, most):
    return max(u for u in range(1, most + 1) if total % u == 0)


def kernel(
    g, near_in, obs_in, cell_in, counts_in, probes, prior, jac, rinv_in, out,
    idx, table, near, obs_row, cell_row, count, rinv,
    blocks, flipped, prior_own, prior_flip, ext_a, ext_b, spread_a, spread_b, weighted_a, weighted_b, adjoint_a, adjoint_b, scan,
    part_obs, got_obs, part_cell, got_cell, part_field, got_field,
    load_sem, fs, fr, ws, wr, os_, or_, gs, gr, cs, cr, es, er,
):
    no, nf, chunk = g["no"], g["nf"], g["chunk"]
    tiles, obs_blocks, nbrs, slots = g["tiles"], g["obs_blocks"], g["nbrs"], g["slots"]
    mine = obs_blocks // nf
    reach = (2 * SIDE + 1) * chunk
    ext, spread = (ext_a, ext_b), (spread_a, spread_b)
    weighted, adjoint = (weighted_a, weighted_b), (adjoint_a, adjoint_b)
    rows = ext_a.shape[1]
    nbr_bits = nbrs.bit_length() - 1
    o = lax.axis_index("obs")
    f = lax.axis_index("flux")
    chunks = no * nf

    def chunk_of(o_, f_):
        odd = lax.rem(f_, 2)
        return odd * (no - 1 - o_) + (1 - odd) * o_

    c = chunk_of(o, f)
    q = f * no + c

    def holder(distance):
        at = lax.rem(q + distance + chunks, chunks)
        f_ = lax.div(at, no)
        return (chunk_of(lax.rem(at, no), f_), f_)

    def flux_peer(r):
        y = g["flux_minor"]
        dz, dy = r
        z_ = lax.rem(lax.div(f, y) + dz, nf // y)
        y_ = lax.rem(lax.rem(f, y) + dy, y)
        return (o, z_ * y + y_)

    def obs_peer(r):
        return (lax.rem(o + r, no), f)

    def hops(d, n):
        return min(d, n - d)

    y = g["flux_minor"]
    far = [(dz, dy) for dz in range(nf // y) for dy in range(y) if dz + dy > 0]
    far.sort(key=lambda r: (-hops(r[0], nf // y) - hops(r[1], y), r))
    around = sorted(range(1, no), key=lambda r: (-hops(r, no), r))
    sides = [d for d in range(-SIDE, SIDE + 1) if d != 0]

    load_jac = pltpu.make_async_copy(jac, blocks, load_sem.at[0])
    load_prior = pltpu.make_async_copy(prior.at[pl.ds(c * chunk, chunk)], prior_own, load_sem.at[1])
    load_field = [
        pltpu.make_async_copy(
            probes.at[pl.ds(c * chunk, chunk), pl.ds(h * rows, rows)],
            ext[h].at[pl.ds(SIDE * chunk, chunk)], load_sem.at[2 + h],
        )
        for h in range(2)
    ]
    small = [(near_in, near), (obs_in, obs_row), (cell_in, cell_row), (counts_in, count), (rinv_in, rinv)]
    load_small = [pltpu.make_async_copy(a, b, load_sem.at[5 + i]) for i, (a, b) in enumerate(small)]
    for copy in load_small + load_field:
        copy.start()
    load_prior.start()
    load_jac.start()

    barrier = pltpu.get_barrier_semaphore()
    partners = [flux_peer(r) for r in far] + [obs_peer(r) for r in around]
    partners += [holder(d) for d in sides]
    for partner in partners:
        pl.semaphore_signal(barrier, inc=1, device_id=partner, device_id_type=MESH)

    pl.semaphore_wait(barrier, len(partners))

    zero = jnp.zeros(spread_a.shape[1:], BF16)
    for h in range(2):
        spread[h][tiles] = zero
        weighted[h][obs_blocks] = zero
        adjoint[h][chunk] = zero

    def remote(src, dst, send, recv, device):
        return pltpu.make_async_remote_copy(
            src_ref=src, dst_ref=dst, send_sem=send, recv_sem=recv, device_id=device, device_id_type=MESH
        )

    def start_all(copies):
        for copy in copies:
            copy.start()

    def field_all(h):
        return remote(*[ext[h].at[pl.ds(0, len(sides) * chunk)]] * 2, es.at[h], er.at[h], holder(1))

    def gather_all(h):
        return remote(*[spread[h].at[pl.ds(0, len(around) * chunk)]] * 2, gs.at[h], gr.at[h], obs_peer(1))

    def predicted_all(h):
        return remote(got_obs.at[h], got_obs.at[h], fs.at[h], fr.at[h], obs_peer(1))

    def weighted_all(h):
        return remote(*[weighted[h].at[pl.ds(0, len(far) * mine)]] * 2, ws.at[h], wr.at[h], obs_peer(1))

    def cell_all(h):
        return remote(got_cell.at[h], got_cell.at[h], os_.at[h], or_.at[h], obs_peer(1))

    def contribution_all(h):
        return remote(got_field.at[h], got_field.at[h], cs.at[h], cr.at[h], obs_peer(1))

    def products(h, base, pairs, lhs_ref, rhs_ref, unroll):
        def one(m, acc):
            a, b = 2 * m, 2 * m + 1
            lhs = jnp.concatenate([lhs_ref[h][idx[base + 1, a]], lhs_ref[h][idx[base + 1, b]]], axis=1)
            rhs = jnp.concatenate([rhs_ref[idx[base, a]], rhs_ref[idx[base, b]]], axis=0)
            acc = acc * idx[base + 2, m].astype(F32)
            acc = acc + jnp.dot(lhs, rhs, preferred_element_type=F32)
            scan[h, m] = acc
            return acc

        def some(i, acc):
            for u in range(unroll):
                acc = one(i * unroll + u, acc)
            return acc

        lax.fori_loop(0, pairs // unroll, some, jnp.zeros(scan.shape[2:], F32))
        scan[h, pairs] = jnp.zeros(scan.shape[2:], F32)

    def last_of(base, segment):
        return idx[base + 2, 2 * LANES + segment]

    def field_copies(h):
        own = ext[h].at[pl.ds(SIDE * chunk, chunk)]
        return [
            remote(own, ext[h].at[pl.ds((SIDE - d) * chunk, chunk)], es.at[h], er.at[h], holder(d))
            for i, d in enumerate(sides)
        ]

    def gather_copies(h):
        own = spread[h].at[pl.ds(c * chunk, chunk)]
        return [remote(own, own, gs.at[h], gr.at[h], obs_peer(r)) for i, r in enumerate(around)]

    def predicted_copies(h):
        copies = []
        for i, r in enumerate(far):
            peer = flux_peer(r)
            part = part_obs.at[h, pl.ds(peer[1] * mine, mine)]
            copies.append(remote(part, got_obs.at[h, i], fs.at[h], fr.at[h], peer))
        return copies

    def weighted_copies(h):
        own = weighted[h].at[pl.ds(f * mine, mine)]
        return [remote(own, own, ws.at[h], wr.at[h], flux_peer(r)) for i, r in enumerate(far)]

    def cell_copies(h):
        copies = []
        for i, r in enumerate(around):
            peer = obs_peer(r)
            part = part_cell.at[h, pl.ds(chunk_of(peer[0], f) * chunk, chunk)]
            copies.append(remote(part, got_cell.at[h, i], os_.at[h], or_.at[h], peer))
        return copies

    def contribution_copies(h):
        return [
            remote(
                part_field.at[h, pl.ds((SIDE + d) * chunk, chunk)], got_field.at[h, i],
                cs.at[h], cr.at[h], holder(d),
            )
            for i, d in enumerate(sides)
        ]

    def spread_phase(h, s):
        every = field_all(h)
        if h == 0:
            @pl.when(s == 0)
            def _():
                load_index.wait()
                load_prior.wait()

        every.wait_recv()
        for t in range(chunk):
            lhs = jnp.concatenate([ext[h][idx[9, t * nbrs + k]] for k in range(nbrs)], axis=1)
            rhs = prior_own[t].reshape(nbrs * prior_own.shape[2], prior_own.shape[3])
            spread[h][c * chunk + t] = jnp.dot(lhs, rhs, preferred_element_type=F32).astype(BF16)
        start_all(gather_copies(h))
        every.wait_send()

    def forward_phase(h, s):
        every = gather_all(h)
        if h == 0:
            @pl.when(s == 0)
            def _():
                for e in range(chunk * nbrs):
                    prior_flip[e] = prior_own[e // nbrs, e % nbrs].T
                load_jac.wait()

        every.wait_recv()
        products(h, 0, g["fwd_pairs"], spread, blocks, g["fwd_unroll"])
        for b in range(obs_blocks):
            part_obs[h, b] = scan[h, last_of(0, b)].astype(BF16)
        start_all(predicted_copies(h))
        every.wait_send()

    def weight_phase(h, s):
        every = predicted_all(h)
        if h == 0:
            @pl.when(s == 0)
            def _():
                many = unroll_of(slots, 8)

                def flip(i, carry):
                    for u in range(many):
                        flipped[i * many + u] = blocks[i * many + u].T
                    return carry

                lax.fori_loop(0, slots // many, flip, 0)

        every.wait_recv()
        for b in range(mine):
            value = scan[h, last_of(0, f * mine + b)]
            for i in range(len(far)):
                value = value + got_obs[h, i, b].astype(F32)
            weighted[h][f * mine + b] = (value * rinv[pl.ds(f * mine + b, 1), :]).astype(BF16)
        start_all(weighted_copies(h))
        every.wait_send()

    def adjoint_phase(h, s):
        every = weighted_all(h)
        every.wait_recv()
        products(h, 3, g["adj_pairs"], weighted, flipped, g["adj_unroll"])
        for t in range(tiles):
            part_cell[h, t] = scan[h, last_of(3, t)].astype(BF16)
        start_all(cell_copies(h))
        every.wait_send()

    def prior_phase(h, s):
        every = cell_all(h)
        every.wait_recv()
        for t in range(chunk):
            value = scan[h, last_of(3, c * chunk + t)]
            for i in range(len(around)):
                value = value + got_cell[h, i, t].astype(F32)
            adjoint[h][t] = value.astype(BF16)
        products(h, 6, g["gat_pairs"], adjoint, prior_flip, g["gat_unroll"])
        for j in range(reach):
            if j // chunk != SIDE:
                part_field[h, j] = scan[h, last_of(6, j)].astype(BF16)
        start_all(contribution_copies(h))
        every.wait_send()

    def field_phase(h, s):
        every = contribution_all(h)
        every.wait_recv()
        for t in range(chunk):
            value = scan[h, last_of(6, SIDE * chunk + t)]
            for i in range(len(sides)):
                value = value + got_field[h, i, t].astype(F32)
            ext[h][SIDE * chunk + t] = value.astype(BF16)

        @pl.when(s < STEPS - 1)
        def _():
            start_all(field_copies(h))

        every.wait_send()

    for h in range(2):
        load_field[h].wait()
        start_all(field_copies(h))

    for copy in load_small:
        copy.wait()
    entry = iota((1, LANES), 1)
    near_row = jnp.zeros((tiles, LANES), jnp.int32)
    by_tile = near[...].T
    for k in range(nbrs):
        here = (iota((tiles, LANES), 0) == c * chunk + (entry >> nbr_bits)) & ((entry & (nbrs - 1)) == k)
        near_row = near_row + jnp.where(here, jnp.broadcast_to(by_tile[:, k : k + 1], here.shape), 0)
    near_row = jnp.clip(total(near_row) - (f * tiles + (c - SIDE) * chunk), 0, reach - 1)
    live = iota((1, slots), 1) < jnp.broadcast_to(count[...], (1, slots))
    by_obs, by_cell = obs_row[0], cell_row[0]
    by_near = jnp.where(entry < chunk * nbrs, near_row, NOBODY)
    segment_pairs(table, 0, jnp.where(live, by_obs, NOBODY), by_cell, tiles, g["fwd_pairs"])
    segment_pairs(table, 3, jnp.where(live, by_cell, NOBODY), by_obs, obs_blocks, g["adj_pairs"])
    segment_pairs(table, 6, by_near, jnp.minimum(entry >> nbr_bits, chunk - 1), chunk, g["gat_pairs"])
    table[9:10, :LANES] = near_row
    load_index = pltpu.make_async_copy(table, idx, load_sem.at[4])
    load_index.start()

    def step(s, carry):
        for phase in (spread_phase, forward_phase, weight_phase, adjoint_phase, prior_phase, field_phase):
            for h in range(2):
                phase(h, s)
        return carry

    lax.fori_loop(0, STEPS, step, 0)
    for h in range(2):
        for t in range(chunk):
            spread[h][c * chunk + t] = ext[h][SIDE * chunk + t]
        start_all(gather_copies(h))
    for h in range(2):
        every = gather_all(h)
        every.wait_recv()
        every.wait_send()
        out[:, pl.ds(h * rows, rows), :] = spread[h][pl.ds(0, tiles)]


def shards(no, nf, flux_minor, probes, prior_tiles, neighbours, jac, jac_obs, jac_flux, counts, rinv):
    tiles, probe_count, width = probes.shape
    nbrs = prior_tiles.shape[1]
    obs_blocks = rinv.shape[0]
    slots = jac.shape[2]
    chunk = tiles // no
    assert SIDE * chunk == REACH and obs_blocks % nf == 0
    reach = (2 * SIDE + 1) * chunk
    fwd_pairs = (slots + obs_blocks) // 2
    adj_pairs = (slots + tiles) // 2
    gat_pairs = (chunk * nbrs + reach) // 2
    assert nbrs & (nbrs - 1) == 0
    assert slots % LANES == 0 and slots < 1024 and max(reach, tiles, obs_blocks) < NOBODY
    assert max(fwd_pairs, adj_pairs) <= 2 * LANES and chunk * nbrs <= LANES
    g = dict(
        no=no, nf=nf, flux_minor=flux_minor, chunk=chunk, tiles=tiles, obs_blocks=obs_blocks, nbrs=nbrs, slots=slots,
        fwd_pairs=fwd_pairs, adj_pairs=adj_pairs, gat_pairs=gat_pairs,
        fwd_unroll=unroll_of(fwd_pairs, 108), adj_unroll=unroll_of(adj_pairs, 108),
        gat_unroll=unroll_of(gat_pairs, 56),
    )
    mine = obs_blocks // nf
    tile = (probe_count, width)
    half = (probe_count // 2, width)
    dma = pltpu.SemaphoreType.DMA
    most = max(fwd_pairs, adj_pairs, gat_pairs) + 1
    vmem = pl.BlockSpec(memory_space=pltpu.VMEM)
    hbm = pl.BlockSpec(memory_space=pltpu.HBM)
    return pl.pallas_call(
        functools.partial(kernel, g),
        out_shape=jax.ShapeDtypeStruct((tiles,) + tile, BF16),
        in_specs=[hbm] * 8,
        out_specs=vmem,
        scratch_shapes=[
            pltpu.SMEM((16, 4 * LANES), jnp.int32),
            pltpu.VMEM((16, 4 * LANES), jnp.int32),
            pltpu.VMEM((nbrs, tiles), jnp.int32),
            pltpu.VMEM((1, 1, slots), jnp.int32),
            pltpu.VMEM((1, 1, slots), jnp.int32),
            pltpu.VMEM((1, 1), jnp.int32),
            pltpu.VMEM((obs_blocks, width), F32),
            pltpu.VMEM((slots, width, width), BF16),
            pltpu.VMEM((slots, width, width), BF16),
            pltpu.VMEM((chunk, nbrs, width, width), BF16),
            pltpu.VMEM((chunk * nbrs, width, width), BF16),
            pltpu.VMEM((reach,) + half, BF16), pltpu.VMEM((reach,) + half, BF16),
            pltpu.VMEM((tiles + 1,) + half, BF16), pltpu.VMEM((tiles + 1,) + half, BF16),
            pltpu.VMEM((obs_blocks + 1,) + half, BF16), pltpu.VMEM((obs_blocks + 1,) + half, BF16),
            pltpu.VMEM((chunk + 1,) + half, BF16), pltpu.VMEM((chunk + 1,) + half, BF16),
            pltpu.VMEM((2, most) + half, F32),
            pltpu.VMEM((2, obs_blocks) + half, BF16),
            pltpu.VMEM((2, nf - 1, mine) + half, BF16),
            pltpu.VMEM((2, tiles) + half, BF16),
            pltpu.VMEM((2, no - 1, chunk) + half, BF16),
            pltpu.VMEM((2, reach) + half, BF16),
            pltpu.VMEM((2, 2 * SIDE, chunk) + half, BF16),
            dma((10,)),
            dma((2,)), dma((2,)), dma((2,)), dma((2,)),
            dma((2,)), dma((2,)), dma((2,)), dma((2,)),
            dma((2,)), dma((2,)), dma((2,)), dma((2,)),
        ],
        compiler_params=pltpu.CompilerParams(
            collective_id=0, has_side_effects=True, vmem_limit_bytes=67043328
        ),
    )(neighbours.T, jac_obs, jac_flux, counts, probes, prior_tiles, jac[0, 0], rinv)


def solution(mesh):
    placed = (
        P("flux", None, None),
        P("flux", None, None, None),
        P("flux", None),
        P("obs", "flux", None, None, None),
        P("obs", "flux", None),
        P("obs", "flux", None),
        P("obs", "flux"),
        P("obs", None),
    )
    return jax.shard_map(
        functools.partial(shards, mesh.shape["obs"], mesh.shape["flux"], FLUX_MINOR),
        mesh=mesh, in_specs=placed, out_specs=P("flux", None, None), check_vma=False,
    )
```

```python
import functools

import jax
import jax.numpy as jnp
from jax import lax
from jax.experimental import pallas as pl
from jax.experimental.pallas import tpu as pltpu
from jax.sharding import PartitionSpec as P

STEPS = 4
REACH = 12
FLUX_MINOR = 4
SIDE = 2
MESH = pl.DeviceIdType.MESH
F32 = jnp.float32
BF16 = jnp.bfloat16


LANES = 128
NOBODY = LANES - 1


def iota(shape, dim):
    return lax.broadcasted_iota(jnp.int32, shape, dim)


def column(row):
    parts = [
        jnp.broadcast_to(row[:, i : i + LANES], (LANES, LANES)).T for i in range(0, row.shape[1], LANES)
    ]
    return jnp.concatenate(parts, axis=0) if len(parts) > 1 else parts[0]


def total(values):
    return jnp.sum(values, axis=0, keepdims=True)


def segment_pairs(table, at, key, lhs, zero_lhs, pairs):
    count = key.shape[1]
    square = (LANES, LANES)
    key_col = column(key)
    size = total((key_col == iota((count, LANES), 1)).astype(jnp.int32))
    even = ((size + 1) >> 1) << 1
    begin = total(jnp.where(iota(square, 0) < iota(square, 1), column(even), 0))
    begin_col, size_col = column(begin), column(size)
    place = []
    for i in range(0, count, LANES):
        here = key[:, i : i + LANES]
        first = total(jnp.where(iota(square, 0) == here, begin_col, 0))
        same = (key_col == here) & (iota((count, LANES), 0) < iota((count, LANES), 1) + i)
        place.append(first + total(same.astype(jnp.int32)))
    place_col = column(jnp.concatenate(place, axis=1) if len(place) > 1 else place[0])
    packed = jnp.where(key_col == NOBODY, 0, (column(lhs) + 1) * 1024 + iota((count, LANES), 0))
    for i in range(0, 2 * pairs, LANES):
        found = total(jnp.where(place_col == iota((count, LANES), 1) + i, packed, 0))
        table[at : at + 1, i : i + LANES] = found & 1023
        table[at + 1 : at + 2, i : i + LANES] = jnp.where(found == 0, zero_lhs, (found >> 10) - 1)
    for i in range(0, 2 * LANES, LANES):
        opens = (begin_col == 2 * (iota(square, 1) + i)) & (size_col > 0)
        table[at + 2 : at + 3, i : i + LANES] = 1 - total(opens.astype(jnp.int32))
    table[at + 2 : at + 3, 2 * LANES : 3 * LANES] = jnp.where(size > 0, ((begin + even) >> 1) - 1, pairs)


def unroll_of(total, most):
    return max(u for u in range(1, most + 1) if total % u == 0)


def kernel(
    g, near_in, obs_in, cell_in, counts_in, probes, prior, jac, rinv_in, out,
    idx, table, near, obs_row, cell_row, count, rinv,
    blocks, flipped, prior_own, prior_flip, ext_a, ext_b, spread_a, spread_b, weighted_a, weighted_b, adjoint_a, adjoint_b, scan,
    part_obs, got_obs, part_cell, got_cell, part_field, got_field,
    load_sem, fs, fr, ws, wr, os_, or_, gs, gr, cs, cr, es, er,
):
    no, nf, chunk = g["no"], g["nf"], g["chunk"]
    tiles, obs_blocks, nbrs, slots = g["tiles"], g["obs_blocks"], g["nbrs"], g["slots"]
    mine = obs_blocks // nf
    reach = (2 * SIDE + 1) * chunk
    ext, spread = (ext_a, ext_b), (spread_a, spread_b)
    weighted, adjoint = (weighted_a, weighted_b), (adjoint_a, adjoint_b)
    rows = ext_a.shape[1]
    nbr_bits = nbrs.bit_length() - 1
    o = lax.axis_index("obs")
    f = lax.axis_index("flux")
    chunks = no * nf

    def chunk_of(o_, f_):
        odd = lax.rem(f_, 2)
        return odd * (no - 1 - o_) + (1 - odd) * o_

    c = chunk_of(o, f)
    q = f * no + c

    def holder(distance):
        at = lax.rem(q + distance + chunks, chunks)
        f_ = lax.div(at, no)
        return (chunk_of(lax.rem(at, no), f_), f_)

    def flux_peer(r):
        y = g["flux_minor"]
        dz, dy = r
        z_ = lax.rem(lax.div(f, y) + dz, nf // y)
        y_ = lax.rem(lax.rem(f, y) + dy, y)
        return (o, z_ * y + y_)

    def obs_peer(r):
        return (lax.rem(o + r, no), f)

    def hops(d, n):
        return min(d, n - d)

    y = g["flux_minor"]
    far = [(dz, dy) for dz in range(nf // y) for dy in range(y) if dz + dy > 0]
    far.sort(key=lambda r: (-hops(r[0], nf // y) - hops(r[1], y), r))
    around = sorted(range(1, no), key=lambda r: (-hops(r, no), r))
    sides = [d for d in range(-SIDE, SIDE + 1) if d != 0]

    load_jac = pltpu.make_async_copy(jac, blocks, load_sem.at[0])
    load_prior = pltpu.make_async_copy(prior.at[pl.ds(c * chunk, chunk)], prior_own, load_sem.at[1])
    load_field = [
        pltpu.make_async_copy(
            probes.at[pl.ds(c * chunk, chunk), pl.ds(h * rows, rows)],
            ext[h].at[pl.ds(SIDE * chunk, chunk)], load_sem.at[2 + h],
        )
        for h in range(2)
    ]
    small = [(near_in, near), (obs_in, obs_row), (cell_in, cell_row), (counts_in, count), (rinv_in, rinv)]
    load_small = [pltpu.make_async_copy(a, b, load_sem.at[5 + i]) for i, (a, b) in enumerate(small)]
    for copy in load_small + load_field:
        copy.start()
    load_prior.start()
    load_jac.start()

    barrier = pltpu.get_barrier_semaphore()
    partners = [flux_peer(r) for r in far] + [obs_peer(r) for r in around]
    partners += [holder(d) for d in sides]
    for partner in partners:
        pl.semaphore_signal(barrier, inc=1, device_id=partner, device_id_type=MESH)

    pl.semaphore_wait(barrier, len(partners))

    zero = jnp.zeros(spread_a.shape[1:], BF16)
    for h in range(2):
        spread[h][tiles] = zero
        weighted[h][obs_blocks] = zero
        adjoint[h][chunk] = zero

    def remote(src, dst, send, recv, device):
        return pltpu.make_async_remote_copy(
            src_ref=src, dst_ref=dst, send_sem=send, recv_sem=recv, device_id=device, device_id_type=MESH
        )

    def start_all(copies):
        for copy in copies:
            copy.start()

    def field_all(h):
        return remote(*[ext[h].at[pl.ds(0, len(sides) * chunk)]] * 2, es.at[h], er.at[h], holder(1))

    def gather_all(h):
        return remote(*[spread[h].at[pl.ds(0, len(around) * chunk)]] * 2, gs.at[h], gr.at[h], obs_peer(1))

    def predicted_all(h):
        return remote(got_obs.at[h], got_obs.at[h], fs.at[h], fr.at[h], obs_peer(1))

    def weighted_all(h):
        return remote(*[weighted[h].at[pl.ds(0, len(far) * mine)]] * 2, ws.at[h], wr.at[h], obs_peer(1))

    def cell_all(h):
        return remote(got_cell.at[h], got_cell.at[h], os_.at[h], or_.at[h], obs_peer(1))

    def contribution_all(h):
        return remote(got_field.at[h], got_field.at[h], cs.at[h], cr.at[h], obs_peer(1))

    def products(h, base, pairs, lhs_ref, rhs_ref, unroll):
        def one(m, acc):
            a, b = 2 * m, 2 * m + 1
            lhs = jnp.concatenate([lhs_ref[h][idx[base + 1, a]], lhs_ref[h][idx[base + 1, b]]], axis=1)
            rhs = jnp.concatenate([rhs_ref[idx[base, a]], rhs_ref[idx[base, b]]], axis=0)
            acc = acc * idx[base + 2, m].astype(F32)
            acc = acc + jnp.dot(lhs, rhs, preferred_element_type=F32)
            scan[h, m] = acc
            return acc

        def some(i, acc):
            for u in range(unroll):
                acc = one(i * unroll + u, acc)
            return acc

        lax.fori_loop(0, pairs // unroll, some, jnp.zeros(scan.shape[2:], F32))
        scan[h, pairs] = jnp.zeros(scan.shape[2:], F32)

    def last_of(base, segment):
        return idx[base + 2, 2 * LANES + segment]

    def field_copies(h):
        own = ext[h].at[pl.ds(SIDE * chunk, chunk)]
        return [
            remote(own, ext[h].at[pl.ds((SIDE - d) * chunk, chunk)], es.at[h], er.at[h], holder(d))
            for i, d in enumerate(sides)
        ]

    def gather_copies(h):
        own = spread[h].at[pl.ds(c * chunk, chunk)]
        return [remote(own, own, gs.at[h], gr.at[h], obs_peer(r)) for i, r in enumerate(around)]

    def predicted_copies(h):
        copies = []
        for i, r in enumerate(far):
            peer = flux_peer(r)
            part = part_obs.at[h, pl.ds(peer[1] * mine, mine)]
            copies.append(remote(part, got_obs.at[h, i], fs.at[h], fr.at[h], peer))
        return copies

    def weighted_copies(h):
        own = weighted[h].at[pl.ds(f * mine, mine)]
        return [remote(own, own, ws.at[h], wr.at[h], flux_peer(r)) for i, r in enumerate(far)]

    def cell_copies(h):
        copies = []
        for i, r in enumerate(around):
            peer = obs_peer(r)
            part = part_cell.at[h, pl.ds(chunk_of(peer[0], f) * chunk, chunk)]
            copies.append(remote(part, got_cell.at[h, i], os_.at[h], or_.at[h], peer))
        return copies

    def contribution_copies(h):
        return [
            remote(
                part_field.at[h, pl.ds((SIDE + d) * chunk, chunk)], got_field.at[h, i],
                cs.at[h], cr.at[h], holder(d),
            )
            for i, d in enumerate(sides)
        ]

    def flip_third(part):
        many = unroll_of(slots // 3, 8)

        def flip(i, carry):
            for u in range(many):
                at = part * (slots // 3) + i * many + u
                flipped[at] = blocks[at].T
            return carry

        lax.fori_loop(0, slots // 3 // many, flip, 0)

    def spread_phase(h, s):
        every = field_all(h)
        if h == 0:
            @pl.when(s == 0)
            def _():
                load_index.wait()
                load_prior.wait()

        every.wait_recv()
        for t in range(chunk):
            lhs = jnp.concatenate([ext[h][idx[9, t * nbrs + k]] for k in range(nbrs)], axis=1)
            rhs = prior_own[t].reshape(nbrs * prior_own.shape[2], prior_own.shape[3])
            spread[h][c * chunk + t] = jnp.dot(lhs, rhs, preferred_element_type=F32).astype(BF16)
        start_all(gather_copies(h))
        every.wait_send()

    def forward_phase(h, s):
        every = gather_all(h)
        if h == 0:
            @pl.when(s == 0)
            def _():
                for e in range(chunk * nbrs):
                    prior_flip[e] = prior_own[e // nbrs, e % nbrs].T
                load_jac.wait()
                flip_third(0)

        every.wait_recv()
        products(h, 0, g["fwd_pairs"], spread, blocks, g["fwd_unroll"])
        for b in range(obs_blocks):
            part_obs[h, b] = scan[h, last_of(0, b)].astype(BF16)
        start_all(predicted_copies(h))
        every.wait_send()

    def weight_phase(h, s):
        every = predicted_all(h)
        if h == 0:
            @pl.when(s == 0)
            def _():
                flip_third(1)

        every.wait_recv()
        for b in range(mine):
            value = scan[h, last_of(0, f * mine + b)]
            for i in range(len(far)):
                value = value + got_obs[h, i, b].astype(F32)
            weighted[h][f * mine + b] = (value * rinv[pl.ds(f * mine + b, 1), :]).astype(BF16)
        start_all(weighted_copies(h))
        every.wait_send()

    def adjoint_phase(h, s):
        every = weighted_all(h)
        if h == 0:
            @pl.when(s == 0)
            def _():
                flip_third(2)

        every.wait_recv()
        products(h, 3, g["adj_pairs"], weighted, flipped, g["adj_unroll"])
        for t in range(tiles):
            part_cell[h, t] = scan[h, last_of(3, t)].astype(BF16)
        start_all(cell_copies(h))
        every.wait_send()

    def prior_phase(h, s):
        every = cell_all(h)
        every.wait_recv()
        for t in range(chunk):
            value = scan[h, last_of(3, c * chunk + t)]
            for i in range(len(around)):
                value = value + got_cell[h, i, t].astype(F32)
            adjoint[h][t] = value.astype(BF16)
        products(h, 6, g["gat_pairs"], adjoint, prior_flip, g["gat_unroll"])
        for j in range(reach):
            if j // chunk != SIDE:
                part_field[h, j] = scan[h, last_of(6, j)].astype(BF16)
        start_all(contribution_copies(h))
        every.wait_send()

    def field_phase(h, s):
        every = contribution_all(h)
        every.wait_recv()
        for t in range(chunk):
            value = scan[h, last_of(6, SIDE * chunk + t)]
            for i in range(len(sides)):
                value = value + got_field[h, i, t].astype(F32)
            ext[h][SIDE * chunk + t] = value.astype(BF16)

        @pl.when(s < STEPS - 1)
        def _():
            start_all(field_copies(h))

        every.wait_send()

    for h in range(2):
        load_field[h].wait()
        start_all(field_copies(h))

    for copy in load_small:
        copy.wait()
    entry = iota((1, LANES), 1)
    near_row = jnp.zeros((tiles, LANES), jnp.int32)
    by_tile = near[...].T
    for k in range(nbrs):
        here = (iota((tiles, LANES), 0) == c * chunk + (entry >> nbr_bits)) & ((entry & (nbrs - 1)) == k)
        near_row = near_row + jnp.where(here, jnp.broadcast_to(by_tile[:, k : k + 1], here.shape), 0)
    near_row = jnp.clip(total(near_row) - (f * tiles + (c - SIDE) * chunk), 0, reach - 1)
    live = iota((1, slots), 1) < jnp.broadcast_to(count[...], (1, slots))
    by_obs, by_cell = obs_row[0], cell_row[0]
    by_near = jnp.where(entry < chunk * nbrs, near_row, NOBODY)
    segment_pairs(table, 0, jnp.where(live, by_obs, NOBODY), by_cell, tiles, g["fwd_pairs"])
    segment_pairs(table, 3, jnp.where(live, by_cell, NOBODY), by_obs, obs_blocks, g["adj_pairs"])
    segment_pairs(table, 6, by_near, jnp.minimum(entry >> nbr_bits, chunk - 1), chunk, g["gat_pairs"])
    table[9:10, :LANES] = near_row
    load_index = pltpu.make_async_copy(table, idx, load_sem.at[4])
    load_index.start()

    def step(s, carry):
        for phase in (spread_phase, forward_phase, weight_phase, adjoint_phase, prior_phase, field_phase):
            for h in range(2):
                phase(h, s)
        return carry

    lax.fori_loop(0, STEPS, step, 0)
    for h in range(2):
        for t in range(chunk):
            spread[h][c * chunk + t] = ext[h][SIDE * chunk + t]
        start_all(gather_copies(h))
    for h in range(2):
        every = gather_all(h)
        every.wait_recv()
        every.wait_send()
        out[:, pl.ds(h * rows, rows), :] = spread[h][pl.ds(0, tiles)]


def shards(no, nf, flux_minor, probes, prior_tiles, neighbours, jac, jac_obs, jac_flux, counts, rinv):
    tiles, probe_count, width = probes.shape
    nbrs = prior_tiles.shape[1]
    obs_blocks = rinv.shape[0]
    slots = jac.shape[2]
    chunk = tiles // no
    assert SIDE * chunk == REACH and obs_blocks % nf == 0
    reach = (2 * SIDE + 1) * chunk
    fwd_pairs = (slots + obs_blocks) // 2
    adj_pairs = (slots + tiles) // 2
    gat_pairs = (chunk * nbrs + reach) // 2
    assert nbrs & (nbrs - 1) == 0
    assert slots % LANES == 0 and slots % 3 == 0 and slots < 1024 and max(reach, tiles, obs_blocks) < NOBODY
    assert max(fwd_pairs, adj_pairs) <= 2 * LANES and chunk * nbrs <= LANES
    g = dict(
        no=no, nf=nf, flux_minor=flux_minor, chunk=chunk, tiles=tiles, obs_blocks=obs_blocks, nbrs=nbrs, slots=slots,
        fwd_pairs=fwd_pairs, adj_pairs=adj_pairs, gat_pairs=gat_pairs,
        fwd_unroll=unroll_of(fwd_pairs, 108), adj_unroll=unroll_of(adj_pairs, 108),
        gat_unroll=unroll_of(gat_pairs, 56),
    )
    mine = obs_blocks // nf
    tile = (probe_count, width)
    half = (probe_count // 2, width)
    dma = pltpu.SemaphoreType.DMA
    most = max(fwd_pairs, adj_pairs, gat_pairs) + 1
    vmem = pl.BlockSpec(memory_space=pltpu.VMEM)
    hbm = pl.BlockSpec(memory_space=pltpu.HBM)
    return pl.pallas_call(
        functools.partial(kernel, g),
        out_shape=jax.ShapeDtypeStruct((tiles,) + tile, BF16),
        in_specs=[hbm] * 8,
        out_specs=vmem,
        scratch_shapes=[
            pltpu.SMEM((16, 4 * LANES), jnp.int32),
            pltpu.VMEM((16, 4 * LANES), jnp.int32),
            pltpu.VMEM((nbrs, tiles), jnp.int32),
            pltpu.VMEM((1, 1, slots), jnp.int32),
            pltpu.VMEM((1, 1, slots), jnp.int32),
            pltpu.VMEM((1, 1), jnp.int32),
            pltpu.VMEM((obs_blocks, width), F32),
            pltpu.VMEM((slots, width, width), BF16),
            pltpu.VMEM((slots, width, width), BF16),
            pltpu.VMEM((chunk, nbrs, width, width), BF16),
            pltpu.VMEM((chunk * nbrs, width, width), BF16),
            pltpu.VMEM((reach,) + half, BF16), pltpu.VMEM((reach,) + half, BF16),
            pltpu.VMEM((tiles + 1,) + half, BF16), pltpu.VMEM((tiles + 1,) + half, BF16),
            pltpu.VMEM((obs_blocks + 1,) + half, BF16), pltpu.VMEM((obs_blocks + 1,) + half, BF16),
            pltpu.VMEM((chunk + 1,) + half, BF16), pltpu.VMEM((chunk + 1,) + half, BF16),
            pltpu.VMEM((2, most) + half, F32),
            pltpu.VMEM((2, obs_blocks) + half, BF16),
            pltpu.VMEM((2, nf - 1, mine) + half, BF16),
            pltpu.VMEM((2, tiles) + half, BF16),
            pltpu.VMEM((2, no - 1, chunk) + half, BF16),
            pltpu.VMEM((2, reach) + half, BF16),
            pltpu.VMEM((2, 2 * SIDE, chunk) + half, BF16),
            dma((10,)),
            dma((2,)), dma((2,)), dma((2,)), dma((2,)),
            dma((2,)), dma((2,)), dma((2,)), dma((2,)),
            dma((2,)), dma((2,)), dma((2,)), dma((2,)),
        ],
        compiler_params=pltpu.CompilerParams(
            collective_id=0, has_side_effects=True, vmem_limit_bytes=67043328
        ),
    )(neighbours.T, jac_obs, jac_flux, counts, probes, prior_tiles, jac[0, 0], rinv)


def solution(mesh):
    placed = (
        P("flux", None, None),
        P("flux", None, None, None),
        P("flux", None),
        P("obs", "flux", None, None, None),
        P("obs", "flux", None),
        P("obs", "flux", None),
        P("obs", "flux"),
        P("obs", None),
    )
    return jax.shard_map(
        functools.partial(shards, mesh.shape["obs"], mesh.shape["flux"], FLUX_MINOR),
        mesh=mesh, in_specs=placed, out_specs=P("flux", None, None), check_vma=False,
    )
```

```python
import functools

import jax
import jax.numpy as jnp
from jax import lax
from jax.experimental import pallas as pl
from jax.experimental.pallas import tpu as pltpu
from jax.sharding import PartitionSpec as P

STEPS = 4
REACH = 12
FLUX_MINOR = 4
SIDE = 2
MESH = pl.DeviceIdType.MESH
F32 = jnp.float32
BF16 = jnp.bfloat16


LANES = 128
NOBODY = LANES - 1


def iota(shape, dim):
    return lax.broadcasted_iota(jnp.int32, shape, dim)


def column(row):
    parts = [
        jnp.broadcast_to(row[:, i : i + LANES], (LANES, LANES)).T for i in range(0, row.shape[1], LANES)
    ]
    return jnp.concatenate(parts, axis=0) if len(parts) > 1 else parts[0]


def total(values):
    return jnp.sum(values, axis=0, keepdims=True)


def segment_pairs(table, at, key, lhs, zero_lhs, pairs):
    count = key.shape[1]
    square = (LANES, LANES)
    key_col = column(key)
    size = total((key_col == iota((count, LANES), 1)).astype(jnp.int32))
    even = ((size + 1) >> 1) << 1
    begin = total(jnp.where(iota(square, 0) < iota(square, 1), column(even), 0))
    begin_col, size_col = column(begin), column(size)
    place = []
    for i in range(0, count, LANES):
        here = key[:, i : i + LANES]
        first = total(jnp.where(iota(square, 0) == here, begin_col, 0))
        same = (key_col == here) & (iota((count, LANES), 0) < iota((count, LANES), 1) + i)
        place.append(first + total(same.astype(jnp.int32)))
    place_col = column(jnp.concatenate(place, axis=1) if len(place) > 1 else place[0])
    packed = jnp.where(key_col == NOBODY, 0, (column(lhs) + 1) * 1024 + iota((count, LANES), 0))
    for i in range(0, 2 * pairs, LANES):
        found = total(jnp.where(place_col == iota((count, LANES), 1) + i, packed, 0))
        table[at : at + 1, i : i + LANES] = found & 1023
        table[at + 1 : at + 2, i : i + LANES] = jnp.where(found == 0, zero_lhs, (found >> 10) - 1)
    for i in range(0, 2 * LANES, LANES):
        opens = (begin_col == 2 * (iota(square, 1) + i)) & (size_col > 0)
        table[at + 2 : at + 3, i : i + LANES] = 1 - total(opens.astype(jnp.int32))
    table[at + 2 : at + 3, 2 * LANES : 3 * LANES] = jnp.where(size > 0, ((begin + even) >> 1) - 1, pairs)


def unroll_of(total, most):
    return max(u for u in range(1, most + 1) if total % u == 0)


def kernel(
    g, near_in, obs_in, cell_in, counts_in, probes, prior, jac, rinv_in, out,
    idx, table, near, obs_row, cell_row, count, rinv,
    blocks, flipped, prior_own, prior_flip, ext_a, ext_b, spread_a, spread_b, weighted_a, weighted_b, adjoint_a, adjoint_b, scan,
    part_obs, got_obs, part_cell, got_cell, part_field, got_field,
    load_sem, fs, fr, ws, wr, os_, or_, gs, gr, cs, cr, es, er,
):
    no, nf, chunk = g["no"], g["nf"], g["chunk"]
    tiles, obs_blocks, nbrs, slots = g["tiles"], g["obs_blocks"], g["nbrs"], g["slots"]
    mine = obs_blocks // nf
    reach = (2 * SIDE + 1) * chunk
    ext, spread = (ext_a, ext_b), (spread_a, spread_b)
    weighted, adjoint = (weighted_a, weighted_b), (adjoint_a, adjoint_b)
    rows = ext_a.shape[1]
    nbr_bits = nbrs.bit_length() - 1
    o = lax.axis_index("obs")
    f = lax.axis_index("flux")
    chunks = no * nf

    def chunk_of(o_, f_):
        odd = lax.rem(f_, 2)
        return odd * (no - 1 - o_) + (1 - odd) * o_

    c = chunk_of(o, f)
    q = f * no + c

    def holder(distance):
        at = lax.rem(q + distance + chunks, chunks)
        f_ = lax.div(at, no)
        return (chunk_of(lax.rem(at, no), f_), f_)

    def flux_peer(r):
        y = g["flux_minor"]
        dz, dy = r
        z_ = lax.rem(lax.div(f, y) + dz, nf // y)
        y_ = lax.rem(lax.rem(f, y) + dy, y)
        return (o, z_ * y + y_)

    def obs_peer(r):
        return (lax.rem(o + r, no), f)

    def hops(d, n):
        return min(d, n - d)

    y = g["flux_minor"]
    far = [(dz, dy) for dz in range(nf // y) for dy in range(y) if dz + dy > 0]
    far.sort(key=lambda r: (-hops(r[0], nf // y) - hops(r[1], y), r))
    around = sorted(range(1, no), key=lambda r: (-hops(r, no), r))
    sides = [d for d in range(-SIDE, SIDE + 1) if d != 0]

    load_jac = pltpu.make_async_copy(jac, blocks, load_sem.at[0])
    load_prior = pltpu.make_async_copy(prior.at[pl.ds(c * chunk, chunk)], prior_own, load_sem.at[1])
    load_field = [
        pltpu.make_async_copy(
            probes.at[pl.ds(c * chunk, chunk), pl.ds(h * rows, rows)],
            ext[h].at[pl.ds(SIDE * chunk, chunk)], load_sem.at[2 + h],
        )
        for h in range(2)
    ]
    small = [(near_in, near), (obs_in, obs_row), (cell_in, cell_row), (counts_in, count), (rinv_in, rinv)]
    load_small = [pltpu.make_async_copy(a, b, load_sem.at[5 + i]) for i, (a, b) in enumerate(small)]
    for copy in load_small + load_field:
        copy.start()
    load_prior.start()
    load_jac.start()

    barrier = pltpu.get_barrier_semaphore()
    partners = [flux_peer(r) for r in far] + [obs_peer(r) for r in around]
    partners += [holder(d) for d in sides]
    for partner in partners:
        pl.semaphore_signal(barrier, inc=1, device_id=partner, device_id_type=MESH)

    pl.semaphore_wait(barrier, len(partners))

    zero = jnp.zeros(spread_a.shape[1:], BF16)
    for h in range(2):
        spread[h][tiles] = zero
        weighted[h][obs_blocks] = zero
        adjoint[h][chunk] = zero

    def remote(src, dst, send, recv, device):
        return pltpu.make_async_remote_copy(
            src_ref=src, dst_ref=dst, send_sem=send, recv_sem=recv, device_id=device, device_id_type=MESH
        )

    def start_all(copies):
        for copy in copies:
            copy.start()

    def field_all(h):
        return remote(*[ext[h].at[pl.ds(0, len(sides) * chunk)]] * 2, es.at[h], er.at[h], holder(1))

    def gather_all(h):
        return remote(*[spread[h].at[pl.ds(0, len(around) * chunk)]] * 2, gs.at[h], gr.at[h], obs_peer(1))

    def predicted_all(h):
        return remote(got_obs.at[h], got_obs.at[h], fs.at[h], fr.at[h], obs_peer(1))

    def weighted_all(h):
        return remote(*[weighted[h].at[pl.ds(0, len(far) * mine)]] * 2, ws.at[h], wr.at[h], obs_peer(1))

    def cell_all(h):
        return remote(got_cell.at[h], got_cell.at[h], os_.at[h], or_.at[h], obs_peer(1))

    def contribution_all(h):
        return remote(got_field.at[h], got_field.at[h], cs.at[h], cr.at[h], obs_peer(1))

    def products(h, base, pairs, lhs_ref, rhs_ref, unroll):
        def one(m, acc):
            a, b = 2 * m, 2 * m + 1
            lhs = jnp.concatenate([lhs_ref[h][idx[base + 1, a]], lhs_ref[h][idx[base + 1, b]]], axis=1)
            rhs = jnp.concatenate([rhs_ref[idx[base, a]], rhs_ref[idx[base, b]]], axis=0)
            acc = acc * idx[base + 2, m].astype(F32)
            acc = acc + jnp.dot(lhs, rhs, preferred_element_type=F32)
            scan[h, m] = acc
            return acc

        def some(i, acc):
            for u in range(unroll):
                acc = one(i * unroll + u, acc)
            return acc

        lax.fori_loop(0, pairs // unroll, some, jnp.zeros(scan.shape[2:], F32))
        scan[h, pairs] = jnp.zeros(scan.shape[2:], F32)

    def last_of(base, segment):
        return idx[base + 2, 2 * LANES + segment]

    def field_copies(h):
        own = ext[h].at[pl.ds(SIDE * chunk, chunk)]
        return [
            remote(own, ext[h].at[pl.ds((SIDE - d) * chunk, chunk)], es.at[h], er.at[h], holder(d))
            for i, d in enumerate(sides)
        ]

    def gather_copies(h):
        own = spread[h].at[pl.ds(c * chunk, chunk)]
        return [remote(own, own, gs.at[h], gr.at[h], obs_peer(r)) for i, r in enumerate(around)]

    def predicted_copies(h):
        copies = []
        for i, r in enumerate(far):
            peer = flux_peer(r)
            part = part_obs.at[h, pl.ds(peer[1] * mine, mine)]
            copies.append(remote(part, got_obs.at[h, i], fs.at[h], fr.at[h], peer))
        return copies

    def weighted_copies(h):
        own = weighted[h].at[pl.ds(f * mine, mine)]
        return [remote(own, own, ws.at[h], wr.at[h], flux_peer(r)) for i, r in enumerate(far)]

    def cell_copies(h):
        copies = []
        for i, r in enumerate(around):
            peer = obs_peer(r)
            part = part_cell.at[h, pl.ds(chunk_of(peer[0], f) * chunk, chunk)]
            copies.append(remote(part, got_cell.at[h, i], os_.at[h], or_.at[h], peer))
        return copies

    def contribution_copies(h):
        return [
            remote(
                part_field.at[h, pl.ds((SIDE + d) * chunk, chunk)], got_field.at[h, i],
                cs.at[h], cr.at[h], holder(d),
            )
            for i, d in enumerate(sides)
        ]

    def flip_third(part):
        many = unroll_of(slots // 3, 8)

        def flip(i, carry):
            for u in range(many):
                at = part * (slots // 3) + i * many + u
                flipped[at] = blocks[at].T
            return carry

        lax.fori_loop(0, slots // 3 // many, flip, 0)

    def spread_phase(h, s):
        every = field_all(h)
        if h == 0:
            @pl.when(s == 0)
            def _():
                load_index.wait()
                load_prior.wait()

        every.wait_recv()
        for t in range(chunk):
            lhs = jnp.concatenate([ext[h][idx[9, t * nbrs + k]] for k in range(nbrs)], axis=1)
            rhs = prior_own[t].reshape(nbrs * prior_own.shape[2], prior_own.shape[3])
            spread[h][c * chunk + t] = jnp.dot(lhs, rhs, preferred_element_type=F32).astype(BF16)
        start_all(gather_copies(h))
        every.wait_send()

    def forward_phase(h, s):
        every = gather_all(h)
        if h == 0:
            @pl.when(s == 0)
            def _():
                for e in range(chunk * nbrs):
                    prior_flip[e] = prior_own[e // nbrs, e % nbrs].T
                load_jac.wait()
                flip_third(0)

        every.wait_recv()
        products(h, 0, g["fwd_pairs"], spread, blocks, g["fwd_unroll"])
        for b in range(obs_blocks):
            part_obs[h, b] = scan[h, last_of(0, b)].astype(BF16)
        start_all(predicted_copies(h))
        every.wait_send()

    def weight_phase(h, s):
        every = predicted_all(h)
        if h == 0:
            @pl.when(s == 0)
            def _():
                flip_third(1)

        every.wait_recv()
        for b in range(mine):
            value = scan[h, last_of(0, f * mine + b)]
            for i in range(len(far)):
                value = value + got_obs[h, i, b].astype(F32)
            weighted[h][f * mine + b] = (value * rinv[pl.ds(f * mine + b, 1), :]).astype(BF16)
        start_all(weighted_copies(h))
        every.wait_send()

    def adjoint_phase(h, s):
        every = weighted_all(h)
        if h == 0:
            @pl.when(s == 0)
            def _():
                flip_third(2)

        every.wait_recv()
        products(h, 3, g["adj_pairs"], weighted, flipped, g["adj_unroll"])
        for t in range(tiles):
            part_cell[h, t] = scan[h, last_of(3, t)].astype(BF16)
        start_all(cell_copies(h))
        every.wait_send()

    def prior_phase(h, s):
        every = cell_all(h)
        every.wait_recv()
        for t in range(chunk):
            value = scan[h, last_of(3, c * chunk + t)]
            for i in range(len(around)):
                value = value + got_cell[h, i, t].astype(F32)
            adjoint[h][t] = value.astype(BF16)
        products(h, 6, g["gat_pairs"], adjoint, prior_flip, g["gat_unroll"])
        for j in range(reach):
            if j // chunk != SIDE:
                part_field[h, j] = scan[h, last_of(6, j)].astype(BF16)
        start_all(contribution_copies(h))
        every.wait_send()

    def field_phase(h, s):
        every = contribution_all(h)
        every.wait_recv()
        for t in range(chunk):
            value = scan[h, last_of(6, SIDE * chunk + t)]
            for i in range(len(sides)):
                value = value + got_field[h, i, t].astype(F32)
            ext[h][SIDE * chunk + t] = value.astype(BF16)

        @pl.when(s < STEPS - 1)
        def _():
            start_all(field_copies(h))

        every.wait_send()

    for h in range(2):
        load_field[h].wait()
        start_all(field_copies(h))

    for copy in load_small:
        copy.wait()
    entry = iota((1, LANES), 1)
    near_row = jnp.zeros((tiles, LANES), jnp.int32)
    by_tile = near[...].T
    for k in range(nbrs):
        here = (iota((tiles, LANES), 0) == c * chunk + (entry >> nbr_bits)) & ((entry & (nbrs - 1)) == k)
        near_row = near_row + jnp.where(here, jnp.broadcast_to(by_tile[:, k : k + 1], here.shape), 0)
    near_row = jnp.clip(total(near_row) - (f * tiles + (c - SIDE) * chunk), 0, reach - 1)
    live = iota((1, slots), 1) < jnp.broadcast_to(count[...], (1, slots))
    by_obs, by_cell = obs_row[0], cell_row[0]
    by_near = jnp.where(entry < chunk * nbrs, near_row, NOBODY)
    segment_pairs(table, 0, jnp.where(live, by_obs, NOBODY), by_cell, tiles, g["fwd_pairs"])
    segment_pairs(table, 3, jnp.where(live, by_cell, NOBODY), by_obs, obs_blocks, g["adj_pairs"])
    segment_pairs(table, 6, by_near, jnp.minimum(entry >> nbr_bits, chunk - 1), chunk, g["gat_pairs"])
    table[9:10, :LANES] = near_row
    load_index = pltpu.make_async_copy(table, idx, load_sem.at[4])
    load_index.start()

    def step(s, carry):
        for phase in (spread_phase, forward_phase, weight_phase, adjoint_phase, prior_phase, field_phase):
            for h in range(2):
                phase(h, s)
        return carry

    lax.fori_loop(0, STEPS, step, 0)
    for h in range(2):
        for t in range(chunk):
            spread[h][c * chunk + t] = ext[h][SIDE * chunk + t]
        start_all(gather_copies(h))
    for h in range(2):
        every = gather_all(h)
        every.wait_recv()
        every.wait_send()
        out[:, pl.ds(h * rows, rows), :] = spread[h][pl.ds(0, tiles)]


def shards(no, nf, flux_minor, probes, prior_tiles, neighbours, jac, jac_obs, jac_flux, counts, rinv):
    tiles, probe_count, width = probes.shape
    nbrs = prior_tiles.shape[1]
    obs_blocks = rinv.shape[0]
    slots = jac.shape[2]
    chunk = tiles // no
    assert SIDE * chunk == REACH and obs_blocks % nf == 0
    reach = (2 * SIDE + 1) * chunk
    fwd_pairs = (slots + obs_blocks) // 2
    adj_pairs = (slots + tiles) // 2
    gat_pairs = (chunk * nbrs + reach) // 2
    assert nbrs & (nbrs - 1) == 0
    assert slots % LANES == 0 and slots % 3 == 0 and slots < 1024 and max(reach, tiles, obs_blocks) < NOBODY
    assert max(fwd_pairs, adj_pairs) <= 2 * LANES and chunk * nbrs <= LANES
    g = dict(
        no=no, nf=nf, flux_minor=flux_minor, chunk=chunk, tiles=tiles, obs_blocks=obs_blocks, nbrs=nbrs, slots=slots,
        fwd_pairs=fwd_pairs, adj_pairs=adj_pairs, gat_pairs=gat_pairs,
        fwd_unroll=unroll_of(fwd_pairs, 108), adj_unroll=unroll_of(adj_pairs, 108),
        gat_unroll=unroll_of(gat_pairs, 56),
    )
    mine = obs_blocks // nf
    tile = (probe_count, width)
    half = (probe_count // 2, width)
    dma = pltpu.SemaphoreType.DMA
    most = max(fwd_pairs, adj_pairs, gat_pairs) + 1
    vmem = pl.BlockSpec(memory_space=pltpu.VMEM)
    hbm = pl.BlockSpec(memory_space=pl.ANY)
    held = functools.partial(pltpu.with_memory_space_constraint, memory_space=pltpu.HBM)
    return pl.pallas_call(
        functools.partial(kernel, g),
        out_shape=jax.ShapeDtypeStruct((tiles,) + tile, BF16),
        in_specs=[hbm] * 8,
        out_specs=vmem,
        scratch_shapes=[
            pltpu.SMEM((16, 4 * LANES), jnp.int32),
            pltpu.VMEM((16, 4 * LANES), jnp.int32),
            pltpu.VMEM((nbrs, tiles), jnp.int32),
            pltpu.VMEM((1, 1, slots), jnp.int32),
            pltpu.VMEM((1, 1, slots), jnp.int32),
            pltpu.VMEM((1, 1), jnp.int32),
            pltpu.VMEM((obs_blocks, width), F32),
            pltpu.VMEM((slots, width, width), BF16),
            pltpu.VMEM((slots, width, width), BF16),
            pltpu.VMEM((chunk, nbrs, width, width), BF16),
            pltpu.VMEM((chunk * nbrs, width, width), BF16),
            pltpu.VMEM((reach,) + half, BF16), pltpu.VMEM((reach,) + half, BF16),
            pltpu.VMEM((tiles + 1,) + half, BF16), pltpu.VMEM((tiles + 1,) + half, BF16),
            pltpu.VMEM((obs_blocks + 1,) + half, BF16), pltpu.VMEM((obs_blocks + 1,) + half, BF16),
            pltpu.VMEM((chunk + 1,) + half, BF16), pltpu.VMEM((chunk + 1,) + half, BF16),
            pltpu.VMEM((2, most) + half, F32),
            pltpu.VMEM((2, obs_blocks) + half, BF16),
            pltpu.VMEM((2, nf - 1, mine) + half, BF16),
            pltpu.VMEM((2, tiles) + half, BF16),
            pltpu.VMEM((2, no - 1, chunk) + half, BF16),
            pltpu.VMEM((2, reach) + half, BF16),
            pltpu.VMEM((2, 2 * SIDE, chunk) + half, BF16),
            dma((10,)),
            dma((2,)), dma((2,)), dma((2,)), dma((2,)),
            dma((2,)), dma((2,)), dma((2,)), dma((2,)),
            dma((2,)), dma((2,)), dma((2,)), dma((2,)),
        ],
        compiler_params=pltpu.CompilerParams(
            collective_id=0, has_side_effects=True, vmem_limit_bytes=48 * 1024 * 1024
        ),
    )(held(neighbours.T), held(jac_obs), held(jac_flux), counts, held(probes), prior_tiles, jac[0, 0], held(rinv))


def solution(mesh):
    placed = (
        P("flux", None, None),
        P("flux", None, None, None),
        P("flux", None),
        P("obs", "flux", None, None, None),
        P("obs", "flux", None),
        P("obs", "flux", None),
        P("obs", "flux"),
        P("obs", None),
    )
    return jax.shard_map(
        functools.partial(shards, mesh.shape["obs"], mesh.shape["flux"], FLUX_MINOR),
        mesh=mesh, in_specs=placed, out_specs=P("flux", None, None), check_vma=False,
    )
```
